32 devices in a mesh: group: 2 (over x), head: 2 (over core), blk: 8 (over z, y).
Axes of the slice: x: 2, y: 2, z: 4, core: 2. Of those that a mesh axis runs over, the one named last changes fastest.
Arguments:
- patches: bfloat16 [4096, 1024], P(('group', 'head', 'blk')), parts along dimension 0, may hold values from -60 to 60
- ln_gain: float32 [1024], replicated, may hold values from 0.1 to 1.9
- w_qkv: bfloat16 [1024, 3072], replicated, may hold values from -0.21875 to 0.21875
- qk_gains: float32 [2, 1024], replicated, may hold values from 0.5 to 6
- w_out: bfloat16 [1024, 1024], replicated, may hold values from -0.1875 to 0.1875
Outputs:
- attn_out: bfloat16 [4096, 1024], P(('group', 'head', 'blk')), parts along dimension 0
The draws below stay inside these ranges and needn't reach their ends.
There are 2 independent parts, one for each index of `group`. The reference program is written for one: setup_inputs(seed, part) draws one part's arguments, and reference() takes and returns one part's arrays. A program takes and returns all parts, laid end to end along the dimension named above; an argument that names none is the same for every part. Nothing has to cross between parts.
All inputs are finite; a program needn't handle non-finite values.
Results may differ from the reference program's by a relative error of at most 0.025.
Values may be sent and summed in bfloat16 or wider, within the bound.
A program may use at most 128 MiB of HBM per device.

```python
import math
import jax
import jax.numpy as jnp
from jax import lax

D = 1024
H = 16
HD = 64
TOKENS = 2048


def draw_patches(key, part):
    key_base = jax.random.fold_in(key, 11)
    base_rows = jax.random.normal(key_base, (TOKENS, D), jnp.float32)
    drawn = jnp.clip(base_rows, -6.0, 6.0)
    return drawn.astype(jnp.bfloat16)


def draw_w_qkv(key, part):
    scale_factor = D ** (-0.5)
    query_part = jnp.clip(jax.random.normal(jax.random.fold_in(key, 21), (D, D), jnp.float32), -6.0, 6.0) * scale_factor
    key_fresh = jnp.clip(jax.random.normal(jax.random.fold_in(key, 22), (D, D), jnp.float32), -6.0, 6.0) * scale_factor
    value_part = jnp.clip(jax.random.normal(jax.random.fold_in(key, 23), (D, D), jnp.float32), -6.0, 6.0) * scale_factor
    key_part = key_fresh
    return jnp.concatenate([query_part, key_part, value_part], axis=1).astype(jnp.bfloat16)


def draw_qk_gains(key, part):
    drawn = jnp.exp(jax.random.uniform(jax.random.fold_in(key, 33), (2, D), jnp.float32, math.log(0.5), math.log(2.5)))
    return drawn.astype(jnp.float32)


def scatter_about(rng, extent, spread, reach, held_as=jnp.bfloat16):
    return jnp.clip(spread * jax.random.normal(rng, extent, jnp.float32), -reach, reach).astype(held_as)


def setup_inputs(seed: int = 0, part: int = 0) -> dict:
    splits = jax.random.split(jax.random.key(seed), 6)
    part_keys = jax.random.split(jax.random.fold_in(splits[5], part), 6)
    patches = draw_patches(jax.random.fold_in(jax.random.fold_in(splits[5], part), 71), part)
    ln_gain = jnp.clip(1.0 + 0.18 * jax.random.normal(splits[1], (D,), jnp.float32), 0.1, 1.9)
    w_qkv = draw_w_qkv(jax.random.fold_in(splits[5], 71), part)
    qk_gains = draw_qk_gains(jax.random.fold_in(splits[5], 71), part)
    w_out = scatter_about(splits[4], (D, D), D ** -0.5, 0.1875)
    return {"patches": patches, "ln_gain": ln_gain, "w_qkv": w_qkv, "qk_gains": qk_gains, "w_out": w_out}


def layer_norm(patches, ln_gain):
    values_f = patches.astype(jnp.float32)
    centre = values_f - lax.optimization_barrier(jnp.mean(values_f, axis=-1, keepdims=True))
    variance = lax.optimization_barrier(jnp.mean(centre * centre, axis=-1, keepdims=True))
    return (centre * lax.rsqrt(variance + 1e-05) * ln_gain).astype(jnp.bfloat16)

def head_norm(columns, gain_vector, head_count):
    row_count = columns.shape[0]
    shaped = columns.reshape(row_count, head_count, HD)
    square_mean = lax.optimization_barrier(jnp.mean(shaped * shaped, axis=-1, keepdims=True))
    scaled = shaped * lax.rsqrt(square_mean + 1e-06) * gain_vector.reshape(head_count, HD)
    return scaled.astype(jnp.bfloat16).reshape(row_count, head_count * HD)

def reference(patches, ln_gain, w_qkv, qk_gains, w_out):
    normed = layer_norm(patches, ln_gain)
    projected = jnp.dot(normed, w_qkv, preferred_element_type=jnp.float32)
    query = head_norm(projected[:, :D], qk_gains[0], H)
    key_rows = head_norm(projected[:, D:2 * D], qk_gains[1], H)
    value_rows = projected[:, 2 * D:].astype(jnp.bfloat16)
    seq_count = patches.shape[0]
    block_rows = 512 if seq_count % 512 == 0 else seq_count
    score_scale = HD ** (-0.5)

    def one_head(triple):
        query_head, key_head, value_head = triple
        query_blocks = query_head.reshape(seq_count // block_rows, block_rows, HD)

        def one_block(query_block):
            scores = jnp.dot(query_block, key_head.T, preferred_element_type=jnp.float32) * score_scale
            row_max = lax.optimization_barrier(jnp.max(scores, axis=-1, keepdims=True))
            exponent = jnp.exp(scores - row_max)
            totals = lax.optimization_barrier(jnp.sum(exponent, axis=-1, keepdims=True))
            summed = jnp.dot(exponent.astype(jnp.bfloat16), value_head, preferred_element_type=jnp.float32)
            return (summed / totals).astype(jnp.bfloat16)
        return lax.map(one_block, query_blocks).reshape(seq_count, HD)

    def by_head(rows_matrix):
        return jnp.transpose(rows_matrix.reshape(seq_count, H, HD), (1, 0, 2))
    attended = lax.map(one_head, (by_head(query), by_head(key_rows), by_head(value_rows)))
    attended = jnp.transpose(attended, (1, 0, 2)).reshape(seq_count, D)
    return jnp.dot(attended, w_out, preferred_element_type=jnp.float32).astype(jnp.bfloat16)
```

```python
import functools
import math

import jax
import jax.numpy as jnp
from jax import lax
from jax.experimental import pallas as pl
from jax.experimental.pallas import tpu as pltpu
from jax.sharding import PartitionSpec as P

H = 16
HD = 64
PARTS = 2
LOG2E = math.log2(math.e)
F32 = jnp.float32
BF16 = jnp.bfloat16


def dot(a, b):
    return jnp.dot(a, b, preferred_element_type=F32)


def dot_nt(a, b):
    return lax.dot_general(a, b, (((1,), (1,)), ((), ())), preferred_element_type=F32)


def kernel(
    n, rows, width,
    patches_hbm, ln_gain_hbm, gains_hbm, w_qkv, w_out, out,
    patches, ln_gain, gains, xg, wq, wk, wv, wvt, wo, qbd, ones, keys, values_t, weights, m_ref, l_ref, acc, att, att_in,
    w_sem, ring_send, ring_recv, sib_send, sib_recv, att_send, att_recv,
):
    d = patches_hbm.shape[1]
    nq = 2 * rows
    half = rows // 2
    sub = half // PARTS
    pairs = width // (2 * HD)
    g, c, b = lax.axis_index("group"), lax.axis_index("head"), lax.axis_index("blk")
    odd = b % 2
    up = jnp.where(b == n - 2, n - 1, b + 2)
    down = jnp.where(b == 1, 0, b - 2)
    nxt = jnp.where(odd == 1, down, up)
    up_p = jnp.where(b == n - 1, n - 2, b + 2)
    down_p = jnp.where(b == 0, 1, b - 2)
    prv = jnp.where(odd == 1, up_p, down_p)
    towards = ((g, c, nxt), (g, c, prv))
    sibling = (g, 1 - c, b)

    small = [
        pltpu.make_async_copy(source, target, w_sem.at[4 + i])
        for i, (source, target) in enumerate(
            ((patches_hbm, patches), (ln_gain_hbm, ln_gain), (gains_hbm, gains))
        )
    ]
    for load in small:
        load.start()
    barrier = pltpu.get_barrier_semaphore()
    for peer in (*towards, sibling):
        pl.semaphore_signal(barrier, inc=1, device_id=peer, device_id_type=pl.DeviceIdType.MESH)

    def fetch(part, target):
        columns = pl.ds(pl.multiple_of(part * d + c * width, 128), width)
        return pltpu.make_async_copy(w_qkv.at[:, columns], target, w_sem.at[part])

    loads = [fetch(0, wq), fetch(1, wk), fetch(2, wv)]
    for load in loads:
        load.start()
    load_out = pltpu.make_async_copy(w_out, wo, w_sem.at[3])
    load_out.start()

    mine = pl.ds(pl.multiple_of(c * rows, rows), rows)
    theirs = pl.ds(pl.multiple_of((1 - c) * rows, rows), rows)

    def piece(k, which, part):
        first = pl.multiple_of(c * rows + which * half + part * sub, sub)
        return xg.at[k, pl.ds(first, sub), :]

    def hop(way, k, part, source):
        return pltpu.make_async_remote_copy(
            src_ref=source,
            dst_ref=piece(k, way, part),
            send_sem=ring_send.at[way, k, part],
            recv_sem=ring_recv.at[way, k, part],
            device_id=towards[way],
            device_id_type=pl.DeviceIdType.MESH,
        )

    def across(k):
        return pltpu.make_async_remote_copy(
            src_ref=xg.at[k, mine, :],
            dst_ref=xg.at[k, mine, :],
            send_sem=sib_send.at[k],
            recv_sem=sib_recv.at[k],
            device_id=sibling,
            device_id_type=pl.DeviceIdType.MESH,
        )

    def across_in(k):
        return pltpu.make_async_remote_copy(
            src_ref=xg.at[k, theirs, :],
            dst_ref=xg.at[k, theirs, :],
            send_sem=sib_send.at[k],
            recv_sem=sib_recv.at[k],
            device_id=sibling,
            device_id_type=pl.DeviceIdType.MESH,
        )

    small[0].wait()
    small[1].wait()
    x = patches[...].astype(F32)
    centre = x - jnp.mean(x, axis=-1, keepdims=True)
    variance = jnp.mean(centre * centre, axis=-1, keepdims=True)
    xg[0, mine, :] = (centre * lax.rsqrt(variance + 1e-05) * ln_gain[...]).astype(BF16)

    pl.semaphore_wait(barrier, 3)
    across(0).start()
    for h in range(2):
        for part in range(PARTS):
            for way in range(2):
                hop(way, 1 + h, part, piece(0, h ^ way, part)).start()

    row_id = lax.broadcasted_iota(jnp.int32, (4 * HD, 4 * HD), 0) >> 6
    col_id = lax.broadcasted_iota(jnp.int32, (4 * HD, 4 * HD), 1) >> 6
    ones[...] = jnp.where(row_id == col_id, 1.0, 0.0).astype(BF16)
    m_ref[...] = jnp.full(m_ref.shape, -1e30, F32)
    l_ref[...] = jnp.zeros(l_ref.shape, F32)
    acc[...] = jnp.zeros(acc.shape, F32)
    qbd[...] = jnp.zeros(qbd.shape, BF16)

    def head_norm(columns, gain):
        parts = []
        for i in range(width // (4 * HD)):
            block = columns[:, i * 4 * HD : (i + 1) * 4 * HD]
            total = dot((block * block).astype(BF16), ones[...])
            parts.append(block * lax.rsqrt(total * (1.0 / HD) + 1e-06))
        return jnp.concatenate(parts, axis=1) * gain

    gain_columns = pl.ds(pl.multiple_of(c * width, 128), width)
    small[2].wait()
    gain_q = gains[0:1, gain_columns]
    gain_k = gains[1:2, gain_columns]

    loads[2].wait()
    wvt[...] = wv[...].T
    loads[0].wait()
    across_in(0).wait_recv()
    query = head_norm(dot(xg[0], wq[...]), gain_q) * (HD ** -0.5 * LOG2E)
    for j in range(pairs):
        block = query[:, j * 2 * HD : (j + 1) * 2 * HD].T.astype(BF16)
        qbd[j, 0:HD, 0:nq] = block[0:HD]
        qbd[j, HD : 2 * HD, nq : 2 * nq] = block[HD : 2 * HD]
    loads[1].wait()

    def absorb_rows(tokens):
        count = tokens.shape[0]
        keys[0:count, :] = head_norm(dot(tokens, wk[...]), gain_k).astype(BF16)
        values_t[:, 0:count] = dot_nt(wvt[...], tokens).astype(BF16)
        shrinks = []
        for j in range(pairs):
            scores = dot(keys[0:count, j * 2 * HD : (j + 1) * 2 * HD], qbd[j])
            old = m_ref[j]
            new = jnp.maximum(old, jnp.max(scores, axis=0, keepdims=True))
            shrink = jnp.exp2(old - new)
            exponent = jnp.exp2(scores - new)
            m_ref[j] = new
            l_ref[j] = l_ref[j] * shrink + jnp.sum(exponent, axis=0, keepdims=True)
            weights[j, 0:count, :] = exponent.astype(BF16)
            shrinks.append(shrink)
        for j in range(pairs):
            for e in range(2):
                channels = slice((2 * j + e) * HD, (2 * j + e + 1) * HD)
                span = slice(e * nq, (e + 1) * nq)
                acc[channels, :] = acc[channels, :] * shrinks[j][:, span] + dot(
                    values_t[channels, 0:count], weights[j, 0:count, span]
                )

    def absorb(k):
        absorb_rows(xg[k])

    def receive(k):
        for part in range(PARTS):
            for way in range(2):
                hop(way, k, part, piece(k, way, part)).wait_recv()

                @pl.when(k < n - 2)
                def _():
                    hop(way, k + 2, part, piece(k, way, part)).start()

        across(k).start()

    def step(k, carry):
        @pl.when((k >= 2) & (k < n - 1))
        def _():
            receive(k)

        @pl.when(k >= 2)
        def _():
            across_in(k - 1).wait_recv()

        absorb(k - 1)

        @pl.when((k == 1) | (k == n - 1))
        def _():
            receive(k)

        return carry

    lax.fori_loop(1, n, step, 0)

    def last(i, carry):
        @pl.when(i == 1)
        def _():
            across_in(n - 1).wait_recv()

        first = (c + i - 2 * c * i) * rows
        absorb_rows(xg[n - 1, pl.ds(pl.multiple_of(first, rows), rows), :])
        return carry

    lax.fori_loop(0, 2, last, 0)

    for j in range(pairs):
        inverse = 1.0 / l_ref[j]
        for e in range(2):
            channels = slice((2 * j + e) * HD, (2 * j + e + 1) * HD)
            acc[channels, :] = acc[channels, :] * inverse[:, e * nq : (e + 1) * nq]
        both = slice(2 * j * HD, 2 * (j + 1) * HD)
        att[:, both] = acc[both, :].T.astype(BF16)
    swap = pltpu.make_async_remote_copy(
        src_ref=att.at[theirs, :],
        dst_ref=att_in,
        send_sem=att_send,
        recv_sem=att_recv,
        device_id=sibling,
        device_id_type=pl.DeviceIdType.MESH,
    )
    swap.start()
    load_out.wait()
    my_heads = pl.ds(pl.multiple_of(c * width, width), width)
    their_heads = pl.ds(pl.multiple_of((1 - c) * width, width), width)
    partial = dot(att[mine, :], wo[my_heads, :])
    swap.wait_recv()
    out[...] = (partial + dot(att_in[...], wo[their_heads, :])).astype(BF16)

    swap.wait_send()
    across(0).wait_send()

    def drain(k, carry):
        for part in range(PARTS):
            for way in range(2):
                hop(way, k, part, piece(k, way, part)).wait_send()
        across(k).wait_send()
        return carry

    lax.fori_loop(1, n, drain, 0)


def per_device(patches, ln_gain, w_qkv, qk_gains, w_out):
    rows, d = patches.shape
    n = lax.axis_size("blk")
    width = H // lax.axis_size("head") * HD
    nq = 2 * rows
    vmem = pl.BlockSpec(memory_space=pltpu.VMEM)
    hbm = pl.BlockSpec(memory_space=pltpu.HBM)
    return pl.pallas_call(
        functools.partial(kernel, n, rows, width),
        out_shape=jax.ShapeDtypeStruct((rows, d), BF16),
        in_specs=[hbm, hbm, hbm, hbm, hbm],
        out_specs=vmem,
        scratch_shapes=[
            pltpu.VMEM((rows, d), BF16),
            pltpu.VMEM((1, d), F32),
            pltpu.VMEM((2, d), F32),
            pltpu.VMEM((n, nq, d), BF16),
            pltpu.VMEM((d, width), BF16),
            pltpu.VMEM((d, width), BF16),
            pltpu.VMEM((d, width), BF16),
            pltpu.VMEM((width, d), BF16),
            pltpu.VMEM((d, d), BF16),
            pltpu.VMEM((width // (2 * HD), 2 * HD, 2 * nq), BF16),
            pltpu.VMEM((4 * HD, 4 * HD), BF16),
            pltpu.VMEM((nq, width), BF16),
            pltpu.VMEM((width, nq), BF16),
            pltpu.VMEM((width // (2 * HD), nq, 2 * nq), BF16),
            pltpu.VMEM((width // (2 * HD), 1, 2 * nq), F32),
            pltpu.VMEM((width // (2 * HD), 1, 2 * nq), F32),
            pltpu.VMEM((width, nq), F32),
            pltpu.VMEM((nq, width), BF16),
            pltpu.VMEM((rows, width), BF16),
            pltpu.SemaphoreType.DMA((7,)),
            pltpu.SemaphoreType.DMA((2, n, PARTS)),
            pltpu.SemaphoreType.DMA((2, n, PARTS)),
            pltpu.SemaphoreType.DMA((n,)),
            pltpu.SemaphoreType.DMA((n,)),
            pltpu.SemaphoreType.DMA,
            pltpu.SemaphoreType.DMA,
        ],
        compiler_params=pltpu.CompilerParams(
            collective_id=0, has_side_effects=True, vmem_limit_bytes=56 << 20
        ),
    )(patches, ln_gain.reshape(1, d), qk_gains, w_qkv, w_out)


def solution(mesh):
    placed = (P(("group", "head", "blk"), None), P(), P(), P(), P())
    return jax.shard_map(
        per_device,
        mesh=mesh,
        in_specs=placed,
        out_specs=P(("group", "head", "blk"), None),
        check_vma=False,
    )
```

```python
import functools
import math

import jax
import jax.numpy as jnp
from jax import lax
from jax.experimental import pallas as pl
from jax.experimental.pallas import tpu as pltpu
from jax.sharding import PartitionSpec as P

H = 16
HD = 64
PARTS = 2
LOG2E = math.log2(math.e)
F32 = jnp.float32
BF16 = jnp.bfloat16


def dot(a, b):
    return jnp.dot(a, b, preferred_element_type=F32)


def dot_nt(a, b):
    return lax.dot_general(a, b, (((1,), (1,)), ((), ())), preferred_element_type=F32)


def kernel(
    n, rows, width,
    patches_hbm, ln_gain_hbm, gains_hbm, w_qkv, w_out, out,
    patches, ln_gain, gains, xg, wq, wk, wv, wvt, wo, qbd, ones, keys, values_t, weights, m_ref, l_ref, acc,
    att, att_in,
    w_sem, ring_send, ring_recv, sib_send, sib_recv, att_send, att_recv,
):
    d = patches_hbm.shape[1]
    nq = 2 * rows
    span = nq // PARTS
    half = span // 2
    sub = half // 2
    pairs = width // (2 * HD)
    items = n * PARTS
    g, c, b = lax.axis_index("group"), lax.axis_index("head"), lax.axis_index("blk")
    odd = b % 2
    up = jnp.where(b == n - 2, n - 1, b + 2)
    down = jnp.where(b == 1, 0, b - 2)
    nxt = jnp.where(odd == 1, down, up)
    up_p = jnp.where(b == n - 1, n - 2, b + 2)
    down_p = jnp.where(b == 0, 1, b - 2)
    prv = jnp.where(odd == 1, up_p, down_p)
    towards = ((g, c, nxt), (g, c, prv))
    sibling = (g, 1 - c, b)

    barrier = pltpu.get_barrier_semaphore()
    for peer in (*towards, sibling):
        pl.semaphore_signal(barrier, inc=1, device_id=peer, device_id_type=pl.DeviceIdType.MESH)
    small = [
        pltpu.make_async_copy(source, target, w_sem.at[4 + i])
        for i, (source, target) in enumerate(
            ((patches_hbm, patches), (ln_gain_hbm, ln_gain), (gains_hbm, gains))
        )
    ]
    for load in small:
        load.start()

    def fetch(part, target):
        columns = pl.ds(pl.multiple_of(part * d + c * width, 128), width)
        return pltpu.make_async_copy(w_qkv.at[:, columns], target, w_sem.at[part])

    loads = [fetch(0, wq), fetch(1, wk), fetch(2, wv)]
    for load in loads:
        load.start()
    load_out = pltpu.make_async_copy(w_out, wo, w_sem.at[3])
    load_out.start()

    mine = pl.ds(pl.multiple_of(c * half, half), half)
    theirs = pl.ds(pl.multiple_of((1 - c) * half, half), half)

    def piece(item, which):
        return xg.at[item, pl.ds(pl.multiple_of(c * half + which * sub, sub), sub), :]

    def hop(way, item, source):
        return pltpu.make_async_remote_copy(
            src_ref=source,
            dst_ref=piece(item, way),
            send_sem=ring_send.at[way, item],
            recv_sem=ring_recv.at[way, item],
            device_id=towards[way],
            device_id_type=pl.DeviceIdType.MESH,
        )

    def exchange(item, place):
        return pltpu.make_async_remote_copy(
            src_ref=xg.at[item, place, :],
            dst_ref=xg.at[item, place, :],
            send_sem=sib_send.at[item],
            recv_sem=sib_recv.at[item],
            device_id=sibling,
            device_id_type=pl.DeviceIdType.MESH,
        )

    def across(item):
        return exchange(item, mine)

    def across_in(item):
        return exchange(item, theirs)

    small[0].wait()
    small[1].wait()
    x = patches[...].astype(F32)
    centre = x - jnp.mean(x, axis=-1, keepdims=True)
    variance = jnp.mean(centre * centre, axis=-1, keepdims=True)
    normed = (centre * lax.rsqrt(variance + 1e-05) * ln_gain[...]).astype(BF16)
    for part in range(PARTS):
        xg[part, mine, :] = normed[part * half : (part + 1) * half]

    pl.semaphore_wait(barrier, 3)
    for part in range(PARTS):
        for way in range(2):
            hop(way, PARTS + part, piece(part, way)).start()
    for part in range(PARTS):
        across(part).start()
    for part in range(PARTS):
        for way in range(2):
            hop(way, 2 * PARTS + part, piece(part, 1 - way)).start()

    row_id = lax.broadcasted_iota(jnp.int32, (4 * HD, 4 * HD), 0) >> 6
    col_id = lax.broadcasted_iota(jnp.int32, (4 * HD, 4 * HD), 1) >> 6
    ones[...] = jnp.where(row_id == col_id, 1.0, 0.0).astype(BF16)
    m_ref[...] = jnp.full(m_ref.shape, -1e30, F32)
    l_ref[...] = jnp.zeros(l_ref.shape, F32)
    acc[...] = jnp.zeros(acc.shape, F32)
    qbd[...] = jnp.zeros(qbd.shape, BF16)

    def head_norm(columns, gain):
        parts = []
        for i in range(width // (4 * HD)):
            block = columns[:, i * 4 * HD : (i + 1) * 4 * HD]
            total = dot((block * block).astype(BF16), ones[...])
            parts.append(block * lax.rsqrt(total * (1.0 / HD) + 1e-06))
        return jnp.concatenate(parts, axis=1) * gain

    gain_columns = pl.ds(pl.multiple_of(c * width, 128), width)
    small[2].wait()
    gain_q = gains[0:1, gain_columns]
    gain_k = gains[1:2, gain_columns]

    loads[2].wait()
    wvt[...] = wv[...].T
    loads[0].wait()
    for part in range(PARTS):
        across_in(part).wait_recv()
    own = jnp.concatenate([xg[part] for part in range(PARTS)], axis=0)
    query = head_norm(dot(own, wq[...]), gain_q) * (HD ** -0.5 * LOG2E)
    for j in range(pairs):
        block = query[:, j * 2 * HD : (j + 1) * 2 * HD].T.astype(BF16)
        qbd[j, 0:HD, 0:nq] = block[0:HD]
        qbd[j, HD : 2 * HD, nq : 2 * nq] = block[HD : 2 * HD]
    loads[1].wait()

    def absorb(item):
        tokens = xg[item]
        keys[...] = head_norm(dot(tokens, wk[...]), gain_k).astype(BF16)
        values_t[...] = dot_nt(wvt[...], tokens).astype(BF16)
        shrinks = []
        for j in range(pairs):
            scores = dot(keys[:, j * 2 * HD : (j + 1) * 2 * HD], qbd[j])
            old = m_ref[j]
            new = jnp.maximum(old, jnp.max(scores, axis=0, keepdims=True))
            shrink = jnp.exp2(old - new)
            exponent = jnp.exp2(scores - new)
            m_ref[j] = new
            l_ref[j] = l_ref[j] * shrink + jnp.sum(exponent, axis=0, keepdims=True)
            weights[j] = exponent.astype(BF16)
            shrinks.append(shrink)
        for j in range(pairs):
            for e in range(2):
                channels = slice((2 * j + e) * HD, (2 * j + e + 1) * HD)
                columns = slice(e * nq, (e + 1) * nq)
                acc[channels, :] = acc[channels, :] * shrinks[j][:, columns] + dot(
                    values_t[channels, :], weights[j, :, columns]
                )

    def receive(item):
        for way in range(2):
            hop(way, item, piece(item, way)).wait_recv()

            @pl.when(item < (n - 2) * PARTS)
            def _():
                hop(way, item + 2 * PARTS, piece(item, way)).start()

        across(item).start()

    def step(t, carry):
        @pl.when(t >= PARTS)
        def _():
            across_in(t).wait_recv()

        absorb(t)

        @pl.when(t < items - PARTS)
        def _():
            receive(t + PARTS)

        return carry

    lax.fori_loop(0, items, step, 0)

    def swap(j):
        return pltpu.make_async_remote_copy(
            src_ref=att.at[j, 1 - c],
            dst_ref=att_in.at[j],
            send_sem=att_send.at[j],
            recv_sem=att_recv.at[j],
            device_id=sibling,
            device_id_type=pl.DeviceIdType.MESH,
        )

    for j in range(pairs):
        inverse = 1.0 / l_ref[j]
        scaled = [
            acc[(2 * j + e) * HD : (2 * j + e + 1) * HD, :] * inverse[:, e * nq : (e + 1) * nq]
            for e in range(2)
        ]
        block = jnp.concatenate(scaled, axis=0).T.astype(BF16)
        for part in range(PARTS):
            for core in range(2):
                first = part * span + core * half
                att[j, core, part * half : (part + 1) * half, :] = block[first : first + half]
        swap(j).start()
    load_out.wait()
    my_heads = pl.ds(pl.multiple_of(c * width, width), width)
    their_heads = pl.ds(pl.multiple_of((1 - c) * width, width), width)
    partial = dot(jnp.concatenate([att[j, c] for j in range(pairs)], axis=1), wo[my_heads, :])
    for j in range(pairs):
        swap(j).wait_recv()
    came = jnp.concatenate([att_in[j] for j in range(pairs)], axis=1)
    out[...] = (partial + dot(came, wo[their_heads, :])).astype(BF16)

    for j in range(pairs):
        swap(j).wait_send()

    def drain(item, carry):
        @pl.when(item >= PARTS)
        def _():
            for way in range(2):
                hop(way, item, piece(item, way)).wait_send()

        across(item).wait_send()
        return carry

    lax.fori_loop(0, items, drain, 0)


def per_device(patches, ln_gain, w_qkv, qk_gains, w_out):
    rows, d = patches.shape
    n = lax.axis_size("blk")
    width = H // lax.axis_size("head") * HD
    nq = 2 * rows
    pairs = width // (2 * HD)
    items = n * PARTS
    span = nq // PARTS
    hbm = pl.BlockSpec(memory_space=pltpu.HBM)
    operands = (patches, ln_gain.reshape(1, d), qk_gains, w_qkv, w_out)
    return pl.pallas_call(
        functools.partial(kernel, n, rows, width),
        out_shape=jax.ShapeDtypeStruct((rows, d), BF16),
        in_specs=[hbm] * len(operands),
        out_specs=pl.BlockSpec(memory_space=pltpu.VMEM),
        scratch_shapes=[
            pltpu.VMEM((rows, d), BF16),
            pltpu.VMEM((1, d), F32),
            pltpu.VMEM((2, d), F32),
            pltpu.VMEM((items, span, d), BF16),
            pltpu.VMEM((d, width), BF16),
            pltpu.VMEM((d, width), BF16),
            pltpu.VMEM((d, width), BF16),
            pltpu.VMEM((width, d), BF16),
            pltpu.VMEM((d, d), BF16),
            pltpu.VMEM((pairs, 2 * HD, 2 * nq), BF16),
            pltpu.VMEM((4 * HD, 4 * HD), BF16),
            pltpu.VMEM((span, width), BF16),
            pltpu.VMEM((width, span), BF16),
            pltpu.VMEM((pairs, span, 2 * nq), BF16),
            pltpu.VMEM((pairs, 1, 2 * nq), F32),
            pltpu.VMEM((pairs, 1, 2 * nq), F32),
            pltpu.VMEM((width, nq), F32),
            pltpu.VMEM((pairs, 2, rows, 2 * HD), BF16),
            pltpu.VMEM((pairs, rows, 2 * HD), BF16),
            pltpu.SemaphoreType.DMA((7,)),
            pltpu.SemaphoreType.DMA((2, items)),
            pltpu.SemaphoreType.DMA((2, items)),
            pltpu.SemaphoreType.DMA((items,)),
            pltpu.SemaphoreType.DMA((items,)),
            pltpu.SemaphoreType.DMA((pairs,)),
            pltpu.SemaphoreType.DMA((pairs,)),
        ],
        compiler_params=pltpu.CompilerParams(
            collective_id=0, has_side_effects=True, vmem_limit_bytes=48 << 20
        ),
    )(*(pltpu.with_memory_space_constraint(a, pltpu.HBM) for a in operands))


def solution(mesh):
    placed = (P(("group", "head", "blk"), None), P(), P(), P(), P())
    return jax.shard_map(
        per_device,
        mesh=mesh,
        in_specs=placed,
        out_specs=P(("group", "head", "blk"), None),
        check_vma=False,
    )
```

```python
import functools
import math

import jax
import jax.numpy as jnp
from jax import lax
from jax.experimental import pallas as pl
from jax.experimental.pallas import tpu as pltpu
from jax.sharding import PartitionSpec as P

HD = 64
PARTS = 2
LOG2E = math.log2(math.e)
F32 = jnp.float32
BF16 = jnp.bfloat16


def dot(a, b):
    return jnp.dot(a, b, preferred_element_type=F32)


def dot_nt(a, b):
    return lax.dot_general(a, b, (((1,), (1,)), ((), ())), preferred_element_type=F32)


def kernel(
    n, rows, d,
    patches_hbm, ln_gain_hbm, gains_hbm, w_qkv, w_out, out,
    patches, ln_gain, gains, xg, xs, wq, wk, wv, wo, qbd, ones, keys, values_t, weights, m_ref, l_ref, acc,
    given, came, given_stats, came_stats,
    w_sem, ring_send, ring_recv, sib_send, sib_recv, merge_send, merge_recv,
):
    nq = 2 * rows
    half = rows // 2
    sub = half // PARTS
    pairs = d // (2 * HD)
    g, c, b = lax.axis_index("group"), lax.axis_index("head"), lax.axis_index("blk")
    odd = b % 2
    up = jnp.where(b == n - 2, n - 1, b + 2)
    down = jnp.where(b == 1, 0, b - 2)
    nxt = jnp.where(odd == 1, down, up)
    up_p = jnp.where(b == n - 1, n - 2, b + 2)
    down_p = jnp.where(b == 0, 1, b - 2)
    prv = jnp.where(odd == 1, up_p, down_p)
    towards = ((g, c, nxt), (g, c, prv))
    sibling = (g, 1 - c, b)

    barrier = pltpu.get_barrier_semaphore()
    for peer in (*towards, sibling):
        pl.semaphore_signal(barrier, inc=1, device_id=peer, device_id_type=pl.DeviceIdType.MESH)
    small = [
        pltpu.make_async_copy(source, target, w_sem.at[4 + i])
        for i, (source, target) in enumerate(
            ((patches_hbm, patches), (ln_gain_hbm, ln_gain), (gains_hbm, gains))
        )
    ]
    loads = [
        pltpu.make_async_copy(w_qkv.at[:, i * d : (i + 1) * d], target, w_sem.at[i])
        for i, target in enumerate((wq, wk, wv))
    ]
    load_out = pltpu.make_async_copy(w_out, wo, w_sem.at[3])
    for load in (*small, *loads, load_out):
        load.start()

    def piece(k, which, part):
        first = which * half + part * sub
        return xg.at[k, first : first + sub, :]

    def hop(way, k, part, source):
        return pltpu.make_async_remote_copy(
            src_ref=source,
            dst_ref=piece(k, way, part),
            send_sem=ring_send.at[way, k, part],
            recv_sem=ring_recv.at[way, k, part],
            device_id=towards[way],
            device_id_type=pl.DeviceIdType.MESH,
        )

    def to_sibling(source, target, send, recv):
        return pltpu.make_async_remote_copy(
            src_ref=source,
            dst_ref=target,
            send_sem=send,
            recv_sem=recv,
            device_id=sibling,
            device_id_type=pl.DeviceIdType.MESH,
        )

    small[0].wait()
    small[1].wait()
    x = patches[...].astype(F32)
    centre = x - jnp.mean(x, axis=-1, keepdims=True)
    variance = jnp.mean(centre * centre, axis=-1, keepdims=True)
    xg[0] = (centre * lax.rsqrt(variance + 1e-05) * ln_gain[...]).astype(BF16)

    pl.semaphore_wait(barrier, 3)
    share = to_sibling(xg.at[0], xs, sib_send, sib_recv)
    for h in range(2):
        for part in range(PARTS):
            for way in range(2):
                hop(way, 1 + h, part, piece(0, h ^ way, part)).start()
        if h == 0:
            share.start()

    row_id = lax.broadcasted_iota(jnp.int32, (4 * HD, 4 * HD), 0) >> 6
    col_id = lax.broadcasted_iota(jnp.int32, (4 * HD, 4 * HD), 1) >> 6
    ones[...] = jnp.where(row_id == col_id, 1.0, 0.0).astype(BF16)
    m_ref[...] = jnp.full(m_ref.shape, -1e30, F32)
    l_ref[...] = jnp.zeros(l_ref.shape, F32)
    acc[...] = jnp.zeros(acc.shape, F32)
    qbd[...] = jnp.zeros(qbd.shape, BF16)

    def head_norm(columns, gain):
        parts = []
        for i in range(d // (4 * HD)):
            block = columns[:, i * 4 * HD : (i + 1) * 4 * HD]
            total = dot((block * block).astype(BF16), ones[...])
            parts.append(block * lax.rsqrt(total * (1.0 / HD) + 1e-06))
        return jnp.concatenate(parts, axis=1) * gain

    small[2].wait()
    loads[0].wait()
    share.wait_recv()
    for which, source in enumerate((xg.at[0], xs)):
        query = head_norm(dot(source[...], wq[...]), gains[0:1, :]) * (HD ** -0.5 * LOG2E)
        for j in range(pairs):
            block = query[:, j * 2 * HD : (j + 1) * 2 * HD].T.astype(BF16)
            for e in range(2):
                first = e * nq + which * rows
                qbd[j, e * HD : (e + 1) * HD, first : first + rows] = block[e * HD : (e + 1) * HD]
    loads[1].wait()
    loads[2].wait()

    def absorb(k, done=None):
        tokens = xg[k]
        keys[...] = head_norm(dot(tokens, wk[...]), gains[1:2, :]).astype(BF16)
        values_t[...] = dot(tokens, wv[...]).astype(BF16).T
        shrinks = []
        for j in range(pairs):
            scores = dot(keys[:, j * 2 * HD : (j + 1) * 2 * HD], qbd[j])
            old = m_ref[j]
            new = jnp.maximum(old, jnp.max(scores, axis=0, keepdims=True))
            shrink = jnp.exp2(old - new)
            exponent = jnp.exp2(scores - new)
            m_ref[j] = new
            l_ref[j] = l_ref[j] * shrink + jnp.sum(exponent, axis=0, keepdims=True)
            weights[j] = exponent.astype(BF16)
            shrinks.append(shrink)
        for j in range(pairs):
            for e in range(2):
                channels = slice((2 * j + e) * HD, (2 * j + e + 1) * HD)
                columns = slice(e * nq, (e + 1) * nq)
                acc[channels, :] = acc[channels, :] * shrinks[j][:, columns] + dot(
                    values_t[channels, :], weights[j, :, columns]
                )
            if done is not None:
                done(j)

    def receive(k):
        for part in range(PARTS):
            for way in range(2):
                hop(way, k, part, piece(k, way, part)).wait_recv()

                @pl.when(k < n - 2)
                def _():
                    hop(way, k + 2, part, piece(k, way, part)).start()

    def step(k, carry):
        absorb(k)
        receive(k + 1)
        return carry

    lax.fori_loop(0, n - 1, step, 0)

    def give(j):
        return to_sibling(given.at[j], came.at[j], merge_send.at[j], merge_recv.at[j])

    give_stats = to_sibling(given_stats, came_stats, merge_send.at[pairs], merge_recv.at[pairs])

    def send_pair(j):
        if j == 0:
            for i in range(pairs):
                for e in range(2):
                    theirs = slice(e * nq + rows, (e + 1) * nq)
                    here = slice(e * rows, (e + 1) * rows)
                    given_stats[0, i, :, here] = m_ref[i, :, theirs]
                    given_stats[1, i, :, here] = l_ref[i, :, theirs]
            give_stats.start()
        both = slice(2 * j * HD, 2 * (j + 1) * HD)
        given[j] = acc[both, rows:nq].astype(BF16)
        give(j).start()

    absorb(n - 1, send_pair)
    load_out.wait()
    give_stats.wait_recv()
    attended = []
    for j in range(pairs):
        give(j).wait_recv()
        heads = []
        for e in range(2):
            mine = slice(e * nq, e * nq + rows)
            here = slice(e * rows, (e + 1) * rows)
            m_own, m_came = m_ref[j, :, mine], came_stats[0, j, :, here]
            m_all = jnp.maximum(m_own, m_came)
            own, other = jnp.exp2(m_own - m_all), jnp.exp2(m_came - m_all)
            inverse = 1.0 / (l_ref[j, :, mine] * own + came_stats[1, j, :, here] * other)
            channels = slice((2 * j + e) * HD, (2 * j + e + 1) * HD)
            heads.append(
                acc[channels, 0:rows] * (own * inverse)
                + came[j, e * HD : (e + 1) * HD, :].astype(F32) * (other * inverse)
            )
        attended.append(jnp.concatenate(heads, axis=0).T.astype(BF16))
    out[...] = dot(jnp.concatenate(attended, axis=1), wo[...]).astype(BF16)

    for j in range(pairs):
        give(j).wait_send()
    give_stats.wait_send()
    share.wait_send()

    def drain(k, carry):
        for part in range(PARTS):
            for way in range(2):
                hop(way, k, part, piece(k, way, part)).wait_send()
        return carry

    lax.fori_loop(1, n, drain, 0)


def per_device(patches, ln_gain, w_qkv, qk_gains, w_out):
    rows, d = patches.shape
    n = lax.axis_size("blk")
    nq = 2 * rows
    pairs = d // (2 * HD)
    hbm = pl.BlockSpec(memory_space=pltpu.HBM)
    operands = (patches, ln_gain.reshape(1, d), qk_gains, w_qkv, w_out)
    return pl.pallas_call(
        functools.partial(kernel, n, rows, d),
        out_shape=jax.ShapeDtypeStruct((rows, d), BF16),
        in_specs=[hbm] * len(operands),
        out_specs=pl.BlockSpec(memory_space=pltpu.VMEM),
        scratch_shapes=[
            pltpu.VMEM((rows, d), BF16),
            pltpu.VMEM((1, d), F32),
            pltpu.VMEM((2, d), F32),
            pltpu.VMEM((n, rows, d), BF16),
            pltpu.VMEM((rows, d), BF16),
            pltpu.VMEM((d, d), BF16),
            pltpu.VMEM((d, d), BF16),
            pltpu.VMEM((d, d), BF16),
            pltpu.VMEM((d, d), BF16),
            pltpu.VMEM((pairs, 2 * HD, 2 * nq), BF16),
            pltpu.VMEM((4 * HD, 4 * HD), BF16),
            pltpu.VMEM((rows, d), BF16),
            pltpu.VMEM((d, rows), BF16),
            pltpu.VMEM((pairs, rows, 2 * nq), BF16),
            pltpu.VMEM((pairs, 1, 2 * nq), F32),
            pltpu.VMEM((pairs, 1, 2 * nq), F32),
            pltpu.VMEM((d, nq), F32),
            pltpu.VMEM((pairs, 2 * HD, rows), BF16),
            pltpu.VMEM((pairs, 2 * HD, rows), BF16),
            pltpu.VMEM((2, pairs, 1, nq), F32),
            pltpu.VMEM((2, pairs, 1, nq), F32),
            pltpu.SemaphoreType.DMA((7,)),
            pltpu.SemaphoreType.DMA((2, n, PARTS)),
            pltpu.SemaphoreType.DMA((2, n, PARTS)),
            pltpu.SemaphoreType.DMA,
            pltpu.SemaphoreType.DMA,
            pltpu.SemaphoreType.DMA((pairs + 1,)),
            pltpu.SemaphoreType.DMA((pairs + 1,)),
        ],
        compiler_params=pltpu.CompilerParams(
            collective_id=0, has_side_effects=True, vmem_limit_bytes=48 << 20
        ),
    )(*(pltpu.with_memory_space_constraint(a, pltpu.HBM) for a in operands))


def solution(mesh):
    placed = (P(("group", "head", "blk"), None), P(), P(), P(), P())
    return jax.shard_map(
        per_device,
        mesh=mesh,
        in_specs=placed,
        out_specs=P(("group", "head", "blk"), None),
        check_vma=False,
    )
```

```python
import functools
import math

import jax
import jax.numpy as jnp
from jax import lax
from jax.experimental import pallas as pl
from jax.experimental.pallas import tpu as pltpu
from jax.sharding import PartitionSpec as P

HD = 64
PARTS = 2
GROUPS = (8,)
LOG2E = math.log2(math.e)
F32 = jnp.float32
BF16 = jnp.bfloat16


def dot(a, b):
    return jnp.dot(a, b, preferred_element_type=F32)


def dot_nt(a, b):
    return lax.dot_general(a, b, (((1,), (1,)), ((), ())), preferred_element_type=F32)


def kernel(
    n, rows, d,
    patches_hbm, ln_gain_hbm, gains_hbm, w_qkv, w_out, out,
    patches, ln_gain, gains, xg, xs, wq, wk, wv, wo, qbd, ones, keys, values_t, weights, m_ref, l_ref, acc,
    given, came, given_stats, came_stats,
    w_sem, ring_send, ring_recv, sib_send, sib_recv, merge_send, merge_recv,
):
    nq = 2 * rows
    half = rows // 2
    sub = half // PARTS
    pairs = d // (2 * HD)
    g, c, b = lax.axis_index("group"), lax.axis_index("head"), lax.axis_index("blk")
    odd = b % 2
    up = jnp.where(b == n - 2, n - 1, b + 2)
    down = jnp.where(b == 1, 0, b - 2)
    nxt = jnp.where(odd == 1, down, up)
    up_p = jnp.where(b == n - 1, n - 2, b + 2)
    down_p = jnp.where(b == 0, 1, b - 2)
    prv = jnp.where(odd == 1, up_p, down_p)
    towards = ((g, c, nxt), (g, c, prv))
    sibling = (g, 1 - c, b)

    barrier = pltpu.get_barrier_semaphore()
    for peer in (*towards, sibling):
        pl.semaphore_signal(barrier, inc=1, device_id=peer, device_id_type=pl.DeviceIdType.MESH)
    small = [
        pltpu.make_async_copy(source, target, w_sem.at[4 + i])
        for i, (source, target) in enumerate(
            ((patches_hbm, patches), (ln_gain_hbm, ln_gain), (gains_hbm, gains))
        )
    ]
    loads = [
        pltpu.make_async_copy(w_qkv.at[:, i * d : (i + 1) * d], target, w_sem.at[i])
        for i, target in enumerate((wq, wk, wv))
    ]
    load_out = pltpu.make_async_copy(w_out, wo, w_sem.at[3])
    for load in (*small, *loads, load_out):
        load.start()

    def piece(k, which, part):
        first = which * half + part * sub
        return xg.at[k, first : first + sub, :]

    def hop(way, k, part, source):
        return pltpu.make_async_remote_copy(
            src_ref=source,
            dst_ref=piece(k, way, part),
            send_sem=ring_send.at[way, k, part],
            recv_sem=ring_recv.at[way, k, part],
            device_id=towards[way],
            device_id_type=pl.DeviceIdType.MESH,
        )

    def to_sibling(source, target, send, recv):
        return pltpu.make_async_remote_copy(
            src_ref=source,
            dst_ref=target,
            send_sem=send,
            recv_sem=recv,
            device_id=sibling,
            device_id_type=pl.DeviceIdType.MESH,
        )

    small[0].wait()
    small[1].wait()
    x = patches[...].astype(F32)
    centre = x - jnp.mean(x, axis=-1, keepdims=True)
    variance = jnp.mean(centre * centre, axis=-1, keepdims=True)
    xg[0] = (centre * lax.rsqrt(variance + 1e-05) * ln_gain[...]).astype(BF16)

    pl.semaphore_wait(barrier, 3)
    share = to_sibling(xg.at[0], xs, sib_send, sib_recv)
    for h in range(2):
        for part in range(PARTS):
            for way in range(2):
                hop(way, 1 + h, part, piece(0, h ^ way, part)).start()
        if h == 0:
            share.start()

    row_id = lax.broadcasted_iota(jnp.int32, (4 * HD, 4 * HD), 0) >> 6
    col_id = lax.broadcasted_iota(jnp.int32, (4 * HD, 4 * HD), 1) >> 6
    ones[...] = jnp.where(row_id == col_id, 1.0, 0.0).astype(BF16)
    m_ref[...] = jnp.full(m_ref.shape, -1e30, F32)
    l_ref[...] = jnp.zeros(l_ref.shape, F32)
    acc[...] = jnp.zeros(acc.shape, F32)
    qbd[...] = jnp.zeros(qbd.shape, BF16)

    def head_norm(columns, gain):
        parts = []
        for i in range(columns.shape[1] // (4 * HD)):
            block = columns[:, i * 4 * HD : (i + 1) * 4 * HD]
            total = dot((block * block).astype(BF16), ones[...])
            parts.append(block * lax.rsqrt(total * (1.0 / HD) + 1e-06))
        return jnp.concatenate(parts, axis=1) * gain

    small[2].wait()
    loads[0].wait()
    share.wait()
    for which, source in enumerate((xg.at[0], xs)):
        query = head_norm(dot(source[...], wq[...]), gains[0:1, :]) * (HD ** -0.5 * LOG2E)
        for j in range(pairs):
            block = query[:, j * 2 * HD : (j + 1) * 2 * HD].T.astype(BF16)
            for e in range(2):
                first = e * nq + which * rows
                qbd[j, e * HD : (e + 1) * HD, first : first + rows] = block[e * HD : (e + 1) * HD]
    loads[1].wait()
    loads[2].wait()

    def project(k):
        tokens = xg[k]
        values_t[...] = dot(tokens, wv[...]).astype(BF16).T
        keys[...] = head_norm(dot(tokens, wk[...]), gains[1:2, :]).astype(BF16)

    def attend(lo, hi, first, last):
        spans = [slice(e * nq + first, e * nq + last) for e in range(2)]
        size = last - first

        def load(ref, j):
            return jnp.concatenate([ref[j, :, span] for span in spans], axis=1)

        shrinks = {}
        for j in range(lo, hi):
            scores = dot(keys[:, j * 2 * HD : (j + 1) * 2 * HD], load(qbd, j))
            old = load(m_ref, j)
            new = jnp.maximum(old, jnp.max(scores, axis=0, keepdims=True))
            shrinks[j] = jnp.exp2(old - new)
            exponent = jnp.exp2(scores - new)
            total = load(l_ref, j) * shrinks[j] + jnp.sum(exponent, axis=0, keepdims=True)
            for e, span in enumerate(spans):
                columns = slice(e * size, (e + 1) * size)
                m_ref[j, :, span] = new[:, columns]
                l_ref[j, :, span] = total[:, columns]
                weights[j, :, span] = exponent[:, columns].astype(BF16)
        for j in range(lo, hi):
            for e, span in enumerate(spans):
                channels = slice((2 * j + e) * HD, (2 * j + e + 1) * HD)
                acc[channels, first:last] = acc[channels, first:last] * shrinks[j][
                    :, e * size : (e + 1) * size
                ] + dot(values_t[channels, :], weights[j, :, span])

    def drain(k):
        for part in range(PARTS):
            for way in range(2):
                hop(way, k, part, piece(k, way, part)).wait_send()

    def receive(k):
        for part in range(PARTS):
            for way in range(2):
                hop(way, k, part, piece(k, way, part)).wait_recv()

                @pl.when(k < n - 2)
                def _():
                    hop(way, k + 2, part, piece(k, way, part)).start()

        @pl.when(k >= 2)
        def _():
            drain(k - 1)

    def step(k, carry):
        project(k)
        attend(0, pairs, 0, nq)
        receive(k + 1)
        return carry

    lax.fori_loop(0, n - 1, step, 0)

    def give(i, lo, hi):
        return (
            to_sibling(
                given_stats.at[lo:hi], came_stats.at[lo:hi], merge_send.at[0, i], merge_recv.at[0, i]
            ),
            to_sibling(given.at[lo:hi], came.at[lo:hi], merge_send.at[1, i], merge_recv.at[1, i]),
        )

    ends = [sum(GROUPS[:i]) * pairs // sum(GROUPS) for i in range(len(GROUPS) + 1)]
    groups = list(zip(ends, ends[1:]))
    project(n - 1)
    for i, (lo, hi) in enumerate(groups):
        attend(lo, hi, rows, nq)
        for j in range(lo, hi):
            for e in range(2):
                theirs = slice(e * nq + rows, (e + 1) * nq)
                here = slice(e * rows, (e + 1) * rows)
                given_stats[j, 0, :, here] = m_ref[j, :, theirs]
                given_stats[j, 1, :, here] = l_ref[j, :, theirs]
            given[j] = acc[2 * j * HD : 2 * (j + 1) * HD, rows:nq].astype(BF16)
        for copy in give(i, lo, hi):
            copy.start()

    attend(0, pairs, 0, rows)
    drain(n - 1)
    load_out.wait()
    total = None
    for i, (lo, hi) in enumerate(groups):
        for copy in give(i, lo, hi):
            copy.wait_recv()
        attended = []
        for j in range(lo, hi):
            heads = []
            for e in range(2):
                mine = slice(e * nq, e * nq + rows)
                here = slice(e * rows, (e + 1) * rows)
                m_own, m_came = m_ref[j, :, mine], came_stats[j, 0, :, here]
                m_all = jnp.maximum(m_own, m_came)
                own, other = jnp.exp2(m_own - m_all), jnp.exp2(m_came - m_all)
                inverse = 1.0 / (l_ref[j, :, mine] * own + came_stats[j, 1, :, here] * other)
                channels = slice((2 * j + e) * HD, (2 * j + e + 1) * HD)
                heads.append(
                    acc[channels, 0:rows] * (own * inverse)
                    + came[j, e * HD : (e + 1) * HD, :].astype(F32) * (other * inverse)
                )
            attended.append(jnp.concatenate(heads, axis=0).T.astype(BF16))
        part = dot(jnp.concatenate(attended, axis=1), wo[2 * lo * HD : 2 * hi * HD, :])
        total = part if total is None else total + part
    out[...] = total.astype(BF16)

    for i, (lo, hi) in enumerate(groups):
        for copy in give(i, lo, hi):
            copy.wait_send()


def per_device(patches, ln_gain, w_qkv, qk_gains, w_out):
    rows, d = patches.shape
    n = lax.axis_size("blk")
    nq = 2 * rows
    pairs = d // (2 * HD)
    hbm = pl.BlockSpec(memory_space=pltpu.HBM)
    operands = (patches, ln_gain.reshape(1, d), qk_gains, w_qkv, w_out)
    return pl.pallas_call(
        functools.partial(kernel, n, rows, d),
        out_shape=jax.ShapeDtypeStruct((rows, d), BF16),
        in_specs=[hbm] * len(operands),
        out_specs=pl.BlockSpec(memory_space=pltpu.VMEM),
        scratch_shapes=[
            pltpu.VMEM((rows, d), BF16),
            pltpu.VMEM((1, d), F32),
            pltpu.VMEM((2, d), F32),
            pltpu.VMEM((n, rows, d), BF16),
            pltpu.VMEM((rows, d), BF16),
            pltpu.VMEM((d, d), BF16),
            pltpu.VMEM((d, d), BF16),
            pltpu.VMEM((d, d), BF16),
            pltpu.VMEM((d, d), BF16),
            pltpu.VMEM((pairs, 2 * HD, 2 * nq), BF16),
            pltpu.VMEM((4 * HD, 4 * HD), BF16),
            pltpu.VMEM((rows, d), BF16),
            pltpu.VMEM((d, rows), BF16),
            pltpu.VMEM((pairs, rows, 2 * nq), BF16),
            pltpu.VMEM((pairs, 1, 2 * nq), F32),
            pltpu.VMEM((pairs, 1, 2 * nq), F32),
            pltpu.VMEM((d, nq), F32),
            pltpu.VMEM((pairs, 2 * HD, rows), BF16),
            pltpu.VMEM((pairs, 2 * HD, rows), BF16),
            pltpu.VMEM((pairs, 2, 1, nq), F32),
            pltpu.VMEM((pairs, 2, 1, nq), F32),
            pltpu.SemaphoreType.DMA((7,)),
            pltpu.SemaphoreType.DMA((2, n, PARTS)),
            pltpu.SemaphoreType.DMA((2, n, PARTS)),
            pltpu.SemaphoreType.DMA,
            pltpu.SemaphoreType.DMA,
            pltpu.SemaphoreType.DMA((2, len(GROUPS))),
            pltpu.SemaphoreType.DMA((2, len(GROUPS))),
        ],
        compiler_params=pltpu.CompilerParams(
            collective_id=0, has_side_effects=True, vmem_limit_bytes=48 << 20
        ),
    )(*(pltpu.with_memory_space_constraint(a, pltpu.HBM) for a in operands))


def solution(mesh):
    placed = (P(("group", "head", "blk"), None), P(), P(), P(), P())
    return jax.shard_map(
        per_device,
        mesh=mesh,
        in_specs=placed,
        out_specs=P(("group", "head", "blk"), None),
        check_vma=False,
    )
```

```python
import functools
import math

import jax
import jax.numpy as jnp
from jax import lax
from jax.experimental import pallas as pl
from jax.experimental.pallas import tpu as pltpu
from jax.sharding import PartitionSpec as P

HD = 64
PARTS = (1, 1)
GROUPS = (8,)
LOG2E = math.log2(math.e)
F32 = jnp.float32
BF16 = jnp.bfloat16


def dot(a, b):
    return jnp.dot(a, b, preferred_element_type=F32)


def dot_nt(a, b):
    return lax.dot_general(a, b, (((1,), (1,)), ((), ())), preferred_element_type=F32)


def kernel(
    n, rows, d,
    patches_hbm, ln_gain_hbm, gains_hbm, w_qkv, w_out, out,
    patches, ln_gain, gains, xg, xs, wq, wk, wv, wo, qbd, ones, keys, values_t, weights, m_ref, l_ref, acc,
    some_keys, some_values, given, came, given_stats, came_stats,
    w_sem, ring_send, ring_recv, sib_send, sib_recv, merge_send, merge_recv,
):
    nq = 2 * rows
    half = rows // 2
    cuts = [sum(PARTS[:i]) * d // sum(PARTS) for i in range(len(PARTS) + 1)]
    pairs = d // (2 * HD)
    g, c, b = lax.axis_index("group"), lax.axis_index("head"), lax.axis_index("blk")
    odd = b % 2
    up = jnp.where(b == n - 2, n - 1, b + 2)
    down = jnp.where(b == 1, 0, b - 2)
    nxt = jnp.where(odd == 1, down, up)
    up_p = jnp.where(b == n - 1, n - 2, b + 2)
    down_p = jnp.where(b == 0, 1, b - 2)
    prv = jnp.where(odd == 1, up_p, down_p)
    towards = ((g, c, nxt), (g, c, prv))
    sibling = (g, 1 - c, b)

    barrier = pltpu.get_barrier_semaphore()
    for peer in (*towards, sibling):
        pl.semaphore_signal(barrier, inc=1, device_id=peer, device_id_type=pl.DeviceIdType.MESH)
    small = [
        pltpu.make_async_copy(source, target, w_sem.at[4 + i])
        for i, (source, target) in enumerate(
            ((patches_hbm, patches), (ln_gain_hbm, ln_gain), (gains_hbm, gains))
        )
    ]
    loads = [
        pltpu.make_async_copy(w_qkv.at[:, i * d : (i + 1) * d], target, w_sem.at[i])
        for i, target in enumerate((wq, wk, wv))
    ]
    load_out = pltpu.make_async_copy(w_out, wo, w_sem.at[3])
    for load in (*small, *loads, load_out):
        load.start()

    def piece(k, which, part):
        return xg.at[k, which * half : (which + 1) * half, cuts[part] : cuts[part + 1]]

    def hop(way, k, part, source):
        return pltpu.make_async_remote_copy(
            src_ref=source,
            dst_ref=piece(k, way, part),
            send_sem=ring_send.at[way, k, part],
            recv_sem=ring_recv.at[way, k, part],
            device_id=towards[way],
            device_id_type=pl.DeviceIdType.MESH,
        )

    def to_sibling(source, target, send, recv):
        return pltpu.make_async_remote_copy(
            src_ref=source,
            dst_ref=target,
            send_sem=send,
            recv_sem=recv,
            device_id=sibling,
            device_id_type=pl.DeviceIdType.MESH,
        )

    small[0].wait()
    small[1].wait()
    x = patches[...].astype(F32)
    centre = x - jnp.mean(x, axis=-1, keepdims=True)
    variance = jnp.mean(centre * centre, axis=-1, keepdims=True)
    xg[0] = (centre * lax.rsqrt(variance + 1e-05) * ln_gain[...]).astype(BF16)

    pl.semaphore_wait(barrier, 3)
    share = to_sibling(xg.at[0], xs, sib_send, sib_recv)
    for h in range(2):
        for part in range(len(PARTS)):
            for way in range(2):
                hop(way, 1 + h, part, piece(0, h ^ way, part)).start()
        if h == 0:
            share.start()

    row_id = lax.broadcasted_iota(jnp.int32, (4 * HD, 4 * HD), 0) >> 6
    col_id = lax.broadcasted_iota(jnp.int32, (4 * HD, 4 * HD), 1) >> 6
    ones[...] = jnp.where(row_id == col_id, 1.0, 0.0).astype(BF16)
    m_ref[...] = jnp.full(m_ref.shape, -1e30, F32)
    l_ref[...] = jnp.zeros(l_ref.shape, F32)
    acc[...] = jnp.zeros(acc.shape, F32)
    qbd[...] = jnp.zeros(qbd.shape, BF16)

    def head_norm(columns, gain):
        parts = []
        for i in range(columns.shape[1] // (4 * HD)):
            block = columns[:, i * 4 * HD : (i + 1) * 4 * HD]
            total = dot((block * block).astype(BF16), ones[...])
            parts.append(block * lax.rsqrt(total * (1.0 / HD) + 1e-06))
        return jnp.concatenate(parts, axis=1) * gain

    small[2].wait()
    loads[0].wait()
    share.wait()
    for which, source in enumerate((xg.at[0], xs)):
        query = head_norm(dot(source[...], wq[...]), gains[0:1, :]) * (HD ** -0.5 * LOG2E)
        for j in range(pairs):
            block = query[:, j * 2 * HD : (j + 1) * 2 * HD].T.astype(BF16)
            for e in range(2):
                first = e * nq + which * rows
                qbd[j, e * HD : (e + 1) * HD, first : first + rows] = block[e * HD : (e + 1) * HD]
    loads[1].wait()
    loads[2].wait()

    def project(k):
        tokens = xg[k]
        values_t[...] = dot(tokens, wv[...]).astype(BF16).T
        keys[...] = head_norm(dot(tokens, wk[...]), gains[1:2, :]).astype(BF16)

    def attend(lo, hi, first, last):
        spans = [slice(e * nq + first, e * nq + last) for e in range(2)]
        size = last - first

        def load(ref, j):
            return jnp.concatenate([ref[j, :, span] for span in spans], axis=1)

        shrinks = {}
        for j in range(lo, hi):
            scores = dot(keys[:, j * 2 * HD : (j + 1) * 2 * HD], load(qbd, j))
            old = load(m_ref, j)
            new = jnp.maximum(old, jnp.max(scores, axis=0, keepdims=True))
            shrinks[j] = jnp.exp2(old - new)
            exponent = jnp.exp2(scores - new)
            total = load(l_ref, j) * shrinks[j] + jnp.sum(exponent, axis=0, keepdims=True)
            for e, span in enumerate(spans):
                columns = slice(e * size, (e + 1) * size)
                m_ref[j, :, span] = new[:, columns]
                l_ref[j, :, span] = total[:, columns]
                weights[j, :, span] = exponent[:, columns].astype(BF16)
        for j in range(lo, hi):
            for e, span in enumerate(spans):
                channels = slice((2 * j + e) * HD, (2 * j + e + 1) * HD)
                acc[channels, first:last] = acc[channels, first:last] * shrinks[j][
                    :, e * size : (e + 1) * size
                ] + dot(values_t[channels, :], weights[j, :, span])

    def drain(k):
        for part in range(len(PARTS)):
            for way in range(2):
                hop(way, k, part, piece(k, way, part)).wait_send()

    def receive(k):
        for part in range(len(PARTS)):

            @pl.when((k < n - 1) | (part < len(PARTS) - 1))
            def _():
                for way in range(2):
                    hop(way, k, part, piece(k, way, part)).wait_recv()

                    @pl.when(k < n - 2)
                    def _():
                        hop(way, k + 2, part, piece(k, way, part)).start()

        @pl.when(k >= 2)
        def _():
            drain(k - 1)

    def step(k, carry):
        project(k)
        attend(0, pairs, 0, nq)
        receive(k + 1)
        return carry

    lax.fori_loop(0, n - 1, step, 0)

    def give(i, lo, hi):
        return (
            to_sibling(
                given_stats.at[lo:hi], came_stats.at[lo:hi], merge_send.at[0, i], merge_recv.at[0, i]
            ),
            to_sibling(given.at[lo:hi], came.at[lo:hi], merge_send.at[1, i], merge_recv.at[1, i]),
        )

    ends = [sum(GROUPS[:i]) * pairs // sum(GROUPS) for i in range(len(GROUPS) + 1)]
    groups = list(zip(ends, ends[1:]))
    early, late = slice(0, cuts[-2]), slice(cuts[-2], d)
    some_values[...] = dot(xg[n - 1, :, early], wv[early, :])
    some_keys[...] = dot(xg[n - 1, :, early], wk[early, :])
    for way in range(2):
        hop(way, n - 1, len(PARTS) - 1, piece(n - 1, way, len(PARTS) - 1)).wait_recv()
    tokens = xg[n - 1, :, late]
    values_t[...] = (some_values[...] + dot(tokens, wv[late, :])).astype(BF16).T
    keys[...] = head_norm(some_keys[...] + dot(tokens, wk[late, :]), gains[1:2, :]).astype(BF16)
    for i, (lo, hi) in enumerate(groups):
        attend(lo, hi, rows, nq)
        for j in range(lo, hi):
            for e in range(2):
                theirs = slice(e * nq + rows, (e + 1) * nq)
                here = slice(e * rows, (e + 1) * rows)
                given_stats[j, 0, :, here] = m_ref[j, :, theirs]
                given_stats[j, 1, :, here] = l_ref[j, :, theirs]
            given[j] = acc[2 * j * HD : 2 * (j + 1) * HD, rows:nq].astype(BF16)
        for copy in give(i, lo, hi):
            copy.start()

    attend(0, pairs, 0, rows)
    drain(n - 1)
    load_out.wait()
    total = None
    for i, (lo, hi) in enumerate(groups):
        for copy in give(i, lo, hi):
            copy.wait_recv()
        attended = []
        for j in range(lo, hi):
            heads = []
            for e in range(2):
                mine = slice(e * nq, e * nq + rows)
                here = slice(e * rows, (e + 1) * rows)
                m_own, m_came = m_ref[j, :, mine], came_stats[j, 0, :, here]
                m_all = jnp.maximum(m_own, m_came)
                own, other = jnp.exp2(m_own - m_all), jnp.exp2(m_came - m_all)
                inverse = 1.0 / (l_ref[j, :, mine] * own + came_stats[j, 1, :, here] * other)
                channels = slice((2 * j + e) * HD, (2 * j + e + 1) * HD)
                heads.append(
                    acc[channels, 0:rows] * (own * inverse)
                    + came[j, e * HD : (e + 1) * HD, :].astype(F32) * (other * inverse)
                )
            attended.append(jnp.concatenate(heads, axis=0).T.astype(BF16))
        part = dot(jnp.concatenate(attended, axis=1), wo[2 * lo * HD : 2 * hi * HD, :])
        total = part if total is None else total + part
    out[...] = total.astype(BF16)

    for i, (lo, hi) in enumerate(groups):
        for copy in give(i, lo, hi):
            copy.wait_send()


def per_device(patches, ln_gain, w_qkv, qk_gains, w_out):
    rows, d = patches.shape
    n = lax.axis_size("blk")
    nq = 2 * rows
    pairs = d // (2 * HD)
    hbm = pl.BlockSpec(memory_space=pltpu.HBM)
    operands = (patches, ln_gain.reshape(1, d), qk_gains, w_qkv, w_out)
    return pl.pallas_call(
        functools.partial(kernel, n, rows, d),
        out_shape=jax.ShapeDtypeStruct((rows, d), BF16),
        in_specs=[hbm] * len(operands),
        out_specs=pl.BlockSpec(memory_space=pltpu.VMEM),
        scratch_shapes=[
            pltpu.VMEM((rows, d), BF16),
            pltpu.VMEM((1, d), F32),
            pltpu.VMEM((2, d), F32),
            pltpu.VMEM((n, rows, d), BF16),
            pltpu.VMEM((rows, d), BF16),
            pltpu.VMEM((d, d), BF16),
            pltpu.VMEM((d, d), BF16),
            pltpu.VMEM((d, d), BF16),
            pltpu.VMEM((d, d), BF16),
            pltpu.VMEM((pairs, 2 * HD, 2 * nq), BF16),
            pltpu.VMEM((4 * HD, 4 * HD), BF16),
            pltpu.VMEM((rows, d), BF16),
            pltpu.VMEM((d, rows), BF16),
            pltpu.VMEM((pairs, rows, 2 * nq), BF16),
            pltpu.VMEM((pairs, 1, 2 * nq), F32),
            pltpu.VMEM((pairs, 1, 2 * nq), F32),
            pltpu.VMEM((d, nq), F32),
            pltpu.VMEM((rows, d), F32),
            pltpu.VMEM((rows, d), F32),
            pltpu.VMEM((pairs, 2 * HD, rows), BF16),
            pltpu.VMEM((pairs, 2 * HD, rows), BF16),
            pltpu.VMEM((pairs, 2, 1, nq), F32),
            pltpu.VMEM((pairs, 2, 1, nq), F32),
            pltpu.SemaphoreType.DMA((7,)),
            pltpu.SemaphoreType.DMA((2, n, len(PARTS))),
            pltpu.SemaphoreType.DMA((2, n, len(PARTS))),
            pltpu.SemaphoreType.DMA,
            pltpu.SemaphoreType.DMA,
            pltpu.SemaphoreType.DMA((2, len(GROUPS))),
            pltpu.SemaphoreType.DMA((2, len(GROUPS))),
        ],
        compiler_params=pltpu.CompilerParams(
            collective_id=0, has_side_effects=True, vmem_limit_bytes=48 << 20
        ),
    )(*(pltpu.with_memory_space_constraint(a, pltpu.HBM) for a in operands))


def solution(mesh):
    placed = (P(("group", "head", "blk"), None), P(), P(), P(), P())
    return jax.shard_map(
        per_device,
        mesh=mesh,
        in_specs=placed,
        out_specs=P(("group", "head", "blk"), None),
        check_vma=False,
    )
```

```python
import functools
import math

import jax
import jax.numpy as jnp
from jax import lax
from jax.experimental import pallas as pl
from jax.experimental.pallas import tpu as pltpu
from jax.sharding import PartitionSpec as P

HD = 64
PARTS = (1, 1)
GROUPS = (8,)
LOG2E = math.log2(math.e)
F32 = jnp.float32
BF16 = jnp.bfloat16


def dot(a, b):
    return jnp.dot(a, b, preferred_element_type=F32)


def dot_nt(a, b):
    return lax.dot_general(a, b, (((1,), (1,)), ((), ())), preferred_element_type=F32)


def kernel(
    n, rows, d,
    patches_hbm, ln_gain_hbm, gains_hbm, w_qkv, w_out, out,
    patches, ln_gain, gains, xg, xs, wq, wk, wv, wo, qbd, ones, keys, values_t, weights, m_ref, l_ref, acc,
    some_keys, some_values, given, came, given_stats, came_stats,
    w_sem, ring_send, ring_recv, sib_send, sib_recv, merge_send, merge_recv,
):
    nq = 2 * rows
    half = rows // 2
    cuts = [sum(PARTS[:i]) * d // sum(PARTS) for i in range(len(PARTS) + 1)]
    pairs = d // (2 * HD)
    g, c, b = lax.axis_index("group"), lax.axis_index("head"), lax.axis_index("blk")
    odd = b % 2
    up = jnp.where(b == n - 2, n - 1, b + 2)
    down = jnp.where(b == 1, 0, b - 2)
    nxt = jnp.where(odd == 1, down, up)
    up_p = jnp.where(b == n - 1, n - 2, b + 2)
    down_p = jnp.where(b == 0, 1, b - 2)
    prv = jnp.where(odd == 1, up_p, down_p)
    towards = ((g, c, nxt), (g, c, prv))
    sibling = (g, 1 - c, b)

    barrier = pltpu.get_barrier_semaphore()
    for peer in (*towards, sibling):
        pl.semaphore_signal(barrier, inc=1, device_id=peer, device_id_type=pl.DeviceIdType.MESH)
    small = [
        pltpu.make_async_copy(source, target, w_sem.at[4 + i])
        for i, (source, target) in enumerate(
            ((patches_hbm, patches), (ln_gain_hbm, ln_gain), (gains_hbm, gains))
        )
    ]
    loads = [
        pltpu.make_async_copy(w_qkv.at[:, i * d : (i + 1) * d], target, w_sem.at[i])
        for i, target in enumerate((wq, wk, wv))
    ]
    load_out = pltpu.make_async_copy(w_out, wo, w_sem.at[3])
    for load in (*small, *loads, load_out):
        load.start()

    def piece(k, which, part):
        return xg.at[k, which * half : (which + 1) * half, cuts[part] : cuts[part + 1]]

    def hop(way, k, part, source):
        return pltpu.make_async_remote_copy(
            src_ref=source,
            dst_ref=piece(k, way, part),
            send_sem=ring_send.at[way, k, part],
            recv_sem=ring_recv.at[way, k, part],
            device_id=towards[way],
            device_id_type=pl.DeviceIdType.MESH,
        )

    def to_sibling(source, target, send, recv):
        return pltpu.make_async_remote_copy(
            src_ref=source,
            dst_ref=target,
            send_sem=send,
            recv_sem=recv,
            device_id=sibling,
            device_id_type=pl.DeviceIdType.MESH,
        )

    small[0].wait()
    small[1].wait()
    x = patches[...].astype(F32)
    centre = x - jnp.mean(x, axis=-1, keepdims=True)
    variance = jnp.mean(centre * centre, axis=-1, keepdims=True)
    xg[0] = (centre * lax.rsqrt(variance + 1e-05) * ln_gain[...]).astype(BF16)

    pl.semaphore_wait(barrier, 3)
    share = to_sibling(xg.at[0], xs, sib_send, sib_recv)
    for h in range(2):
        for part in range(len(PARTS)):
            for way in range(2):
                hop(way, 1 + h, part, piece(0, h ^ way, part)).start()
        if h == 0:
            share.start()

    row_id = lax.broadcasted_iota(jnp.int32, (4 * HD, 4 * HD), 0) >> 6
    col_id = lax.broadcasted_iota(jnp.int32, (4 * HD, 4 * HD), 1) >> 6
    ones[...] = jnp.where(row_id == col_id, 1.0, 0.0).astype(BF16)
    m_ref[...] = jnp.full(m_ref.shape, -1e30, F32)
    l_ref[...] = jnp.zeros(l_ref.shape, F32)
    acc[...] = jnp.zeros(acc.shape, F32)
    qbd[...] = jnp.zeros(qbd.shape, BF16)

    def head_norm(columns, gain):
        parts = []
        for i in range(columns.shape[1] // (4 * HD)):
            block = columns[:, i * 4 * HD : (i + 1) * 4 * HD]
            total = dot((block * block).astype(BF16), ones[...])
            parts.append(block * lax.rsqrt(total * (1.0 / HD) + 1e-06))
        return jnp.concatenate(parts, axis=1) * gain

    small[2].wait()
    loads[0].wait()
    share.wait()
    for which, source in enumerate((xg.at[0], xs)):
        query = head_norm(dot(source[...], wq[...]), gains[0:1, :]) * (HD ** -0.5 * LOG2E)
        for j in range(pairs):
            block = query[:, j * 2 * HD : (j + 1) * 2 * HD].T.astype(BF16)
            for e in range(2):
                first = e * nq + which * rows
                qbd[j, e * HD : (e + 1) * HD, first : first + rows] = block[e * HD : (e + 1) * HD]
    loads[1].wait()
    loads[2].wait()

    def project(k):
        tokens = xg[k]
        values_t[...] = dot(tokens, wv[...]).astype(BF16).T
        keys[...] = head_norm(dot(tokens, wk[...]), gains[1:2, :]).astype(BF16)

    def attend(lo, hi, first, last):
        spans = [slice(e * nq + first, e * nq + last) for e in range(2)]
        size = last - first

        def load(ref, j):
            return jnp.concatenate([ref[j, :, span] for span in spans], axis=1)

        shrinks = {}
        for j in range(lo, hi):
            scores = dot(keys[:, j * 2 * HD : (j + 1) * 2 * HD], load(qbd, j))
            old = load(m_ref, j)
            new = jnp.maximum(old, jnp.max(scores, axis=0, keepdims=True))
            shrinks[j] = jnp.exp2(old - new)
            exponent = jnp.exp2(scores - new)
            total = load(l_ref, j) * shrinks[j] + jnp.sum(exponent, axis=0, keepdims=True)
            for e, span in enumerate(spans):
                columns = slice(e * size, (e + 1) * size)
                m_ref[j, :, span] = new[:, columns]
                l_ref[j, :, span] = total[:, columns]
                weights[j, :, span] = exponent[:, columns].astype(BF16)
        for j in range(lo, hi):
            both = slice(2 * j * HD, 2 * (j + 1) * HD)
            joint = dot(values_t[both, :], load(weights, j)) if size <= 2 * HD else None
            for e, span in enumerate(spans):
                channels = slice((2 * j + e) * HD, (2 * j + e + 1) * HD)
                columns = slice(e * size, (e + 1) * size)
                if joint is None:
                    term = dot(values_t[channels, :], weights[j, :, span])
                else:
                    term = joint[e * HD : (e + 1) * HD, columns]
                acc[channels, first:last] = (
                    acc[channels, first:last] * shrinks[j][:, columns] + term
                )

    def drain(k):
        for part in range(len(PARTS)):
            for way in range(2):
                hop(way, k, part, piece(k, way, part)).wait_send()

    def receive(k):
        for part in range(len(PARTS)):

            @pl.when((k < n - 1) | (part < len(PARTS) - 1))
            def _():
                for way in range(2):
                    hop(way, k, part, piece(k, way, part)).wait_recv()

                    @pl.when(k < n - 2)
                    def _():
                        hop(way, k + 2, part, piece(k, way, part)).start()

        @pl.when(k >= 2)
        def _():
            drain(k - 1)

    def step(k, carry):
        project(k)
        attend(0, pairs, 0, nq)
        receive(k + 1)
        return carry

    lax.fori_loop(0, n - 1, step, 0)

    def give(i, lo, hi):
        return (
            to_sibling(
                given_stats.at[lo:hi], came_stats.at[lo:hi], merge_send.at[0, i], merge_recv.at[0, i]
            ),
            to_sibling(given.at[lo:hi], came.at[lo:hi], merge_send.at[1, i], merge_recv.at[1, i]),
        )

    ends = [sum(GROUPS[:i]) * pairs // sum(GROUPS) for i in range(len(GROUPS) + 1)]
    groups = list(zip(ends, ends[1:]))
    early, late = slice(0, cuts[-2]), slice(cuts[-2], d)
    some_values[...] = dot(xg[n - 1, :, early], wv[early, :])
    some_keys[...] = dot(xg[n - 1, :, early], wk[early, :])
    for way in range(2):
        hop(way, n - 1, len(PARTS) - 1, piece(n - 1, way, len(PARTS) - 1)).wait_recv()
    tokens = xg[n - 1, :, late]
    keys[...] = head_norm(some_keys[...] + dot(tokens, wk[late, :]), gains[1:2, :]).astype(BF16)
    values_t[...] = (some_values[...] + dot(tokens, wv[late, :])).astype(BF16).T
    for i, (lo, hi) in enumerate(groups):
        attend(lo, hi, rows, nq)
        for j in range(lo, hi):
            for e in range(2):
                theirs = slice(e * nq + rows, (e + 1) * nq)
                here = slice(e * rows, (e + 1) * rows)
                given_stats[j, 0, :, here] = m_ref[j, :, theirs]
                given_stats[j, 1, :, here] = l_ref[j, :, theirs]
            given[j] = acc[2 * j * HD : 2 * (j + 1) * HD, rows:nq].astype(BF16)
        for copy in give(i, lo, hi):
            copy.start()

    attend(0, pairs, 0, rows)
    drain(n - 1)
    load_out.wait()
    total = None
    for i, (lo, hi) in enumerate(groups):
        for copy in give(i, lo, hi):
            copy.wait_recv()
        attended = []
        for j in range(lo, hi):
            heads = []
            for e in range(2):
                mine = slice(e * nq, e * nq + rows)
                here = slice(e * rows, (e + 1) * rows)
                m_own, m_came = m_ref[j, :, mine], came_stats[j, 0, :, here]
                m_all = jnp.maximum(m_own, m_came)
                own, other = jnp.exp2(m_own - m_all), jnp.exp2(m_came - m_all)
                inverse = 1.0 / (l_ref[j, :, mine] * own + came_stats[j, 1, :, here] * other)
                channels = slice((2 * j + e) * HD, (2 * j + e + 1) * HD)
                heads.append(
                    acc[channels, 0:rows] * (own * inverse)
                    + came[j, e * HD : (e + 1) * HD, :].astype(F32) * (other * inverse)
                )
            attended.append(jnp.concatenate(heads, axis=0).T.astype(BF16))
        part = dot(jnp.concatenate(attended, axis=1), wo[2 * lo * HD : 2 * hi * HD, :])
        total = part if total is None else total + part
    out[...] = total.astype(BF16)

    for i, (lo, hi) in enumerate(groups):
        for copy in give(i, lo, hi):
            copy.wait_send()


def per_device(patches, ln_gain, w_qkv, qk_gains, w_out):
    rows, d = patches.shape
    n = lax.axis_size("blk")
    nq = 2 * rows
    pairs = d // (2 * HD)
    hbm = pl.BlockSpec(memory_space=pltpu.HBM)
    operands = (patches, ln_gain.reshape(1, d), qk_gains, w_qkv, w_out)
    return pl.pallas_call(
        functools.partial(kernel, n, rows, d),
        out_shape=jax.ShapeDtypeStruct((rows, d), BF16),
        in_specs=[hbm] * len(operands),
        out_specs=pl.BlockSpec(memory_space=pltpu.VMEM),
        scratch_shapes=[
            pltpu.VMEM((rows, d), BF16),
            pltpu.VMEM((1, d), F32),
            pltpu.VMEM((2, d), F32),
            pltpu.VMEM((n, rows, d), BF16),
            pltpu.VMEM((rows, d), BF16),
            pltpu.VMEM((d, d), BF16),
            pltpu.VMEM((d, d), BF16),
            pltpu.VMEM((d, d), BF16),
            pltpu.VMEM((d, d), BF16),
            pltpu.VMEM((pairs, 2 * HD, 2 * nq), BF16),
            pltpu.VMEM((4 * HD, 4 * HD), BF16),
            pltpu.VMEM((rows, d), BF16),
            pltpu.VMEM((d, rows), BF16),
            pltpu.VMEM((pairs, rows, 2 * nq), BF16),
            pltpu.VMEM((pairs, 1, 2 * nq), F32),
            pltpu.VMEM((pairs, 1, 2 * nq), F32),
            pltpu.VMEM((d, nq), F32),
            pltpu.VMEM((rows, d), F32),
            pltpu.VMEM((rows, d), F32),
            pltpu.VMEM((pairs, 2 * HD, rows), BF16),
            pltpu.VMEM((pairs, 2 * HD, rows), BF16),
            pltpu.VMEM((pairs, 2, 1, nq), F32),
            pltpu.VMEM((pairs, 2, 1, nq), F32),
            pltpu.SemaphoreType.DMA((7,)),
            pltpu.SemaphoreType.DMA((2, n, len(PARTS))),
            pltpu.SemaphoreType.DMA((2, n, len(PARTS))),
            pltpu.SemaphoreType.DMA,
            pltpu.SemaphoreType.DMA,
            pltpu.SemaphoreType.DMA((2, len(GROUPS))),
            pltpu.SemaphoreType.DMA((2, len(GROUPS))),
        ],
        compiler_params=pltpu.CompilerParams(
            collective_id=0, has_side_effects=True, vmem_limit_bytes=48 << 20
        ),
    )(*(pltpu.with_memory_space_constraint(a, pltpu.HBM) for a in operands))


def solution(mesh):
    placed = (P(("group", "head", "blk"), None), P(), P(), P(), P())
    return jax.shard_map(
        per_device,
        mesh=mesh,
        in_specs=placed,
        out_specs=P(("group", "head", "blk"), None),
        check_vma=False,
    )
```

```python
import functools
import math

import jax
import jax.numpy as jnp
from jax import lax
from jax.experimental import pallas as pl
from jax.experimental.pallas import tpu as pltpu
from jax.sharding import PartitionSpec as P

HD = 64
PARTS = (1, 1)
GROUPS = (8,)
LOG2E = math.log2(math.e)
F32 = jnp.float32
BF16 = jnp.bfloat16


def dot(a, b):
    return jnp.dot(a, b, preferred_element_type=F32)


def dot_nt(a, b):
    return lax.dot_general(a, b, (((1,), (1,)), ((), ())), preferred_element_type=F32)


def kernel(
    n, rows, d,
    patches_hbm, ln_gain_hbm, gains_hbm, w_qkv, w_out, out,
    patches, ln_gain, gains, xg, xs, wq, wk, wv, wo, qbd, ones, keys, values_t, weights, m_ref, l_ref, acc,
    some_keys, some_values, given, came, given_stats, came_stats,
    w_sem, ring_send, ring_recv, sib_send, sib_recv, merge_send, merge_recv,
):
    nq = 2 * rows
    half = rows // 2
    cuts = [sum(PARTS[:i]) * d // sum(PARTS) for i in range(len(PARTS) + 1)]
    pairs = d // (2 * HD)
    g, c, b = lax.axis_index("group"), lax.axis_index("head"), lax.axis_index("blk")
    odd = b % 2
    up = jnp.where(b == n - 2, n - 1, b + 2)
    down = jnp.where(b == 1, 0, b - 2)
    nxt = jnp.where(odd == 1, down, up)
    up_p = jnp.where(b == n - 1, n - 2, b + 2)
    down_p = jnp.where(b == 0, 1, b - 2)
    prv = jnp.where(odd == 1, up_p, down_p)
    towards = ((g, c, nxt), (g, c, prv))
    sibling = (g, 1 - c, b)

    barrier = pltpu.get_barrier_semaphore()
    for peer in (*towards, sibling):
        pl.semaphore_signal(barrier, inc=1, device_id=peer, device_id_type=pl.DeviceIdType.MESH)
    small = [
        pltpu.make_async_copy(source, target, w_sem.at[4 + i])
        for i, (source, target) in enumerate(
            ((patches_hbm, patches), (ln_gain_hbm, ln_gain), (gains_hbm, gains))
        )
    ]
    loads = [
        pltpu.make_async_copy(w_qkv.at[:, i * d : (i + 1) * d], target, w_sem.at[i])
        for i, target in enumerate((wq, wk, wv))
    ]
    load_out = pltpu.make_async_copy(w_out, wo, w_sem.at[3])
    for load in (*small, *loads, load_out):
        load.start()

    def piece(k, which, part):
        return xg.at[k, which * half : (which + 1) * half, cuts[part] : cuts[part + 1]]

    def hop(way, k, part, source):
        return pltpu.make_async_remote_copy(
            src_ref=source,
            dst_ref=piece(k, way, part),
            send_sem=ring_send.at[way, k, part],
            recv_sem=ring_recv.at[way, k, part],
            device_id=towards[way],
            device_id_type=pl.DeviceIdType.MESH,
        )

    def to_sibling(source, target, send, recv):
        return pltpu.make_async_remote_copy(
            src_ref=source,
            dst_ref=target,
            send_sem=send,
            recv_sem=recv,
            device_id=sibling,
            device_id_type=pl.DeviceIdType.MESH,
        )

    small[0].wait()
    small[1].wait()
    x = patches[...].astype(F32)
    centre = x - jnp.mean(x, axis=-1, keepdims=True)
    variance = jnp.mean(centre * centre, axis=-1, keepdims=True)
    xg[0] = (centre * lax.rsqrt(variance + 1e-05) * ln_gain[...]).astype(BF16)

    pl.semaphore_wait(barrier, 3)
    share = to_sibling(xg.at[0], xs, sib_send, sib_recv)
    for h in range(2):
        for part in range(len(PARTS)):
            for way in range(2):
                hop(way, 1 + h, part, piece(0, h ^ way, part)).start()
        if h == 0:
            share.start()

    row_id = lax.broadcasted_iota(jnp.int32, (4 * HD, 4 * HD), 0) >> 6
    col_id = lax.broadcasted_iota(jnp.int32, (4 * HD, 4 * HD), 1) >> 6
    ones[...] = jnp.where(row_id == col_id, 1.0, 0.0).astype(BF16)
    m_ref[...] = jnp.full(m_ref.shape, -1e30, F32)
    l_ref[...] = jnp.zeros(l_ref.shape, F32)
    acc[...] = jnp.zeros(acc.shape, F32)
    qbd[...] = jnp.zeros(qbd.shape, BF16)

    def head_norm(columns, gain):
        parts = []
        for i in range(columns.shape[1] // (4 * HD)):
            block = columns[:, i * 4 * HD : (i + 1) * 4 * HD]
            total = dot((block * block).astype(BF16), ones[...])
            parts.append(block * lax.rsqrt(total * (1.0 / HD) + 1e-06))
        return jnp.concatenate(parts, axis=1) * gain

    small[2].wait()
    loads[0].wait()
    share.wait()
    for which, source in enumerate((xg.at[0], xs)):
        query = head_norm(dot(source[...], wq[...]), gains[0:1, :]) * (HD ** -0.5 * LOG2E)
        for j in range(pairs):
            block = query[:, j * 2 * HD : (j + 1) * 2 * HD].T.astype(BF16)
            for e in range(2):
                first = e * nq + which * rows
                qbd[j, e * HD : (e + 1) * HD, first : first + rows] = block[e * HD : (e + 1) * HD]
    loads[1].wait()
    loads[2].wait()

    def project(k):
        tokens = xg[k]
        values_t[...] = dot(tokens, wv[...]).astype(BF16).T
        keys[...] = head_norm(dot(tokens, wk[...]), gains[1:2, :]).astype(BF16)

    def attend(lo, hi, first, last, giving=False):
        spans = [slice(e * nq + first, e * nq + last) for e in range(2)]
        size = last - first

        def load(ref, j):
            return jnp.concatenate([ref[j, :, span] for span in spans], axis=1)

        shrinks = {}
        for j in range(lo, hi):
            scores = dot(keys[:, j * 2 * HD : (j + 1) * 2 * HD], load(qbd, j))
            old = load(m_ref, j)
            new = jnp.maximum(old, jnp.max(scores, axis=0, keepdims=True))
            shrinks[j] = jnp.exp2(old - new)
            exponent = jnp.exp2(scores - new)
            total = load(l_ref, j) * shrinks[j] + jnp.sum(exponent, axis=0, keepdims=True)
            for e, span in enumerate(spans):
                columns = slice(e * size, (e + 1) * size)
                if giving:
                    given_stats[j, 0, :, columns] = new[:, columns]
                    given_stats[j, 1, :, columns] = total[:, columns]
                else:
                    m_ref[j, :, span] = new[:, columns]
                    l_ref[j, :, span] = total[:, columns]
                weights[j, :, span] = exponent[:, columns].astype(BF16)
        for j in range(lo, hi):
            both = slice(2 * j * HD, 2 * (j + 1) * HD)
            joint = dot(values_t[both, :], load(weights, j)) if size <= 2 * HD else None
            for e, span in enumerate(spans):
                channels = slice((2 * j + e) * HD, (2 * j + e + 1) * HD)
                columns = slice(e * size, (e + 1) * size)
                if joint is None:
                    term = dot(values_t[channels, :], weights[j, :, span])
                else:
                    term = joint[e * HD : (e + 1) * HD, columns]
                value = acc[channels, first:last] * shrinks[j][:, columns] + term
                if giving:
                    given[j, e * HD : (e + 1) * HD, :] = value.astype(BF16)
                else:
                    acc[channels, first:last] = value

    def drain(k):
        for part in range(len(PARTS)):
            for way in range(2):
                hop(way, k, part, piece(k, way, part)).wait_send()

    def receive(k):
        for part in range(len(PARTS)):

            @pl.when((k < n - 1) | (part < len(PARTS) - 1))
            def _():
                for way in range(2):
                    hop(way, k, part, piece(k, way, part)).wait_recv()

                    @pl.when(k < n - 2)
                    def _():
                        hop(way, k + 2, part, piece(k, way, part)).start()

        @pl.when(k >= 2)
        def _():
            drain(k - 1)

    def step(k, carry):
        project(k)
        attend(0, pairs, 0, nq)
        receive(k + 1)
        return carry

    lax.fori_loop(0, n - 1, step, 0)

    def give(i, lo, hi):
        return (
            to_sibling(
                given_stats.at[lo:hi], came_stats.at[lo:hi], merge_send.at[0, i], merge_recv.at[0, i]
            ),
            to_sibling(given.at[lo:hi], came.at[lo:hi], merge_send.at[1, i], merge_recv.at[1, i]),
        )

    ends = [sum(GROUPS[:i]) * pairs // sum(GROUPS) for i in range(len(GROUPS) + 1)]
    groups = list(zip(ends, ends[1:]))
    early, late = slice(0, cuts[-2]), slice(cuts[-2], d)
    some_values[...] = dot(xg[n - 1, :, early], wv[early, :])
    some_keys[...] = dot(xg[n - 1, :, early], wk[early, :])
    for way in range(2):
        hop(way, n - 1, len(PARTS) - 1, piece(n - 1, way, len(PARTS) - 1)).wait_recv()
    tokens = xg[n - 1, :, late]
    keys[...] = head_norm(some_keys[...] + dot(tokens, wk[late, :]), gains[1:2, :]).astype(BF16)
    values_t[...] = (some_values[...] + dot(tokens, wv[late, :])).astype(BF16).T
    for i, (lo, hi) in enumerate(groups):
        attend(lo, hi, rows, nq, giving=True)
        for copy in give(i, lo, hi):
            copy.start()

    attend(0, pairs, 0, rows)
    drain(n - 1)
    load_out.wait()
    total = None
    for i, (lo, hi) in enumerate(groups):
        for copy in give(i, lo, hi):
            copy.wait_recv()
        attended = []
        for j in range(lo, hi):
            heads = []
            for e in range(2):
                mine = slice(e * nq, e * nq + rows)
                here = slice(e * rows, (e + 1) * rows)
                m_own, m_came = m_ref[j, :, mine], came_stats[j, 0, :, here]
                m_all = jnp.maximum(m_own, m_came)
                own, other = jnp.exp2(m_own - m_all), jnp.exp2(m_came - m_all)
                inverse = 1.0 / (l_ref[j, :, mine] * own + came_stats[j, 1, :, here] * other)
                channels = slice((2 * j + e) * HD, (2 * j + e + 1) * HD)
                heads.append(
                    acc[channels, 0:rows] * (own * inverse)
                    + came[j, e * HD : (e + 1) * HD, :].astype(F32) * (other * inverse)
                )
            attended.append(jnp.concatenate(heads, axis=0).T.astype(BF16))
        part = dot(jnp.concatenate(attended, axis=1), wo[2 * lo * HD : 2 * hi * HD, :])
        total = part if total is None else total + part
    out[...] = total.astype(BF16)

    for i, (lo, hi) in enumerate(groups):
        for copy in give(i, lo, hi):
            copy.wait_send()


def per_device(patches, ln_gain, w_qkv, qk_gains, w_out):
    rows, d = patches.shape
    n = lax.axis_size("blk")
    nq = 2 * rows
    pairs = d // (2 * HD)
    hbm = pl.BlockSpec(memory_space=pltpu.HBM)
    operands = (patches, ln_gain.reshape(1, d), qk_gains, w_qkv, w_out)
    return pl.pallas_call(
        functools.partial(kernel, n, rows, d),
        out_shape=jax.ShapeDtypeStruct((rows, d), BF16),
        in_specs=[hbm] * len(operands),
        out_specs=pl.BlockSpec(memory_space=pltpu.VMEM),
        scratch_shapes=[
            pltpu.VMEM((rows, d), BF16),
            pltpu.VMEM((1, d), F32),
            pltpu.VMEM((2, d), F32),
            pltpu.VMEM((n, rows, d), BF16),
            pltpu.VMEM((rows, d), BF16),
            pltpu.VMEM((d, d), BF16),
            pltpu.VMEM((d, d), BF16),
            pltpu.VMEM((d, d), BF16),
            pltpu.VMEM((d, d), BF16),
            pltpu.VMEM((pairs, 2 * HD, 2 * nq), BF16),
            pltpu.VMEM((4 * HD, 4 * HD), BF16),
            pltpu.VMEM((rows, d), BF16),
            pltpu.VMEM((d, rows), BF16),
            pltpu.VMEM((pairs, rows, 2 * nq), BF16),
            pltpu.VMEM((pairs, 1, 2 * nq), F32),
            pltpu.VMEM((pairs, 1, 2 * nq), F32),
            pltpu.VMEM((d, nq), F32),
            pltpu.VMEM((rows, d), F32),
            pltpu.VMEM((rows, d), F32),
            pltpu.VMEM((pairs, 2 * HD, rows), BF16),
            pltpu.VMEM((pairs, 2 * HD, rows), BF16),
            pltpu.VMEM((pairs, 2, 1, nq), F32),
            pltpu.VMEM((pairs, 2, 1, nq), F32),
            pltpu.SemaphoreType.DMA((7,)),
            pltpu.SemaphoreType.DMA((2, n, len(PARTS))),
            pltpu.SemaphoreType.DMA((2, n, len(PARTS))),
            pltpu.SemaphoreType.DMA,
            pltpu.SemaphoreType.DMA,
            pltpu.SemaphoreType.DMA((2, len(GROUPS))),
            pltpu.SemaphoreType.DMA((2, len(GROUPS))),
        ],
        compiler_params=pltpu.CompilerParams(
            collective_id=0, has_side_effects=True, vmem_limit_bytes=48 << 20
        ),
    )(*(pltpu.with_memory_space_constraint(a, pltpu.HBM) for a in operands))


def solution(mesh):
    placed = (P(("group", "head", "blk"), None), P(), P(), P(), P())
    return jax.shard_map(
        per_device,
        mesh=mesh,
        in_specs=placed,
        out_specs=P(("group", "head", "blk"), None),
        check_vma=False,
    )
```

```python
import functools
import math

import jax
import jax.numpy as jnp
from jax import lax
from jax.experimental import pallas as pl
from jax.experimental.pallas import tpu as pltpu
from jax.sharding import PartitionSpec as P

HD = 64
PARTS = (1, 1)
GROUPS = (8,)
LOG2E = math.log2(math.e)
F32 = jnp.float32
BF16 = jnp.bfloat16


def dot(a, b):
    return jnp.dot(a, b, preferred_element_type=F32)


def dot_nt(a, b):
    return lax.dot_general(a, b, (((1,), (1,)), ((), ())), preferred_element_type=F32)


def kernel(
    n, rows, d,
    patches_hbm, ln_gain_hbm, gains_hbm, w_qkv, w_out, out,
    patches, ln_gain, gains, xg, xs, wq, wk, wv, wo, qbd, ones, keys, values_t, weights, m_ref, l_ref, acc,
    some_keys, some_values, given, came, given_stats, came_stats,
    w_sem, ring_send, ring_recv, sib_send, sib_recv, merge_send, merge_recv,
):
    nq = 2 * rows
    half = rows // 2
    cuts = [sum(PARTS[:i]) * d // sum(PARTS) for i in range(len(PARTS) + 1)]
    pairs = d // (2 * HD)
    g, c, b = lax.axis_index("group"), lax.axis_index("head"), lax.axis_index("blk")
    odd = b % 2
    up = jnp.where(b == n - 2, n - 1, b + 2)
    down = jnp.where(b == 1, 0, b - 2)
    nxt = jnp.where(odd == 1, down, up)
    up_p = jnp.where(b == n - 1, n - 2, b + 2)
    down_p = jnp.where(b == 0, 1, b - 2)
    prv = jnp.where(odd == 1, up_p, down_p)
    towards = ((g, c, nxt), (g, c, prv))
    sibling = (g, 1 - c, b)

    barrier = pltpu.get_barrier_semaphore()
    for peer in (*towards, sibling):
        pl.semaphore_signal(barrier, inc=1, device_id=peer, device_id_type=pl.DeviceIdType.MESH)
    small = [
        pltpu.make_async_copy(source, target, w_sem.at[4 + i])
        for i, (source, target) in enumerate(
            ((patches_hbm, patches), (ln_gain_hbm, ln_gain), (gains_hbm, gains))
        )
    ]
    loads = [
        pltpu.make_async_copy(w_qkv.at[:, i * d : (i + 1) * d], target, w_sem.at[i])
        for i, target in enumerate((wq, wk, wv))
    ]
    load_out = pltpu.make_async_copy(w_out, wo, w_sem.at[3])
    for load in (*small, *loads, load_out):
        load.start()

    def piece(k, which, part):
        return xg.at[k, which * half : (which + 1) * half, cuts[part] : cuts[part + 1]]

    def hop(way, k, part, source):
        return pltpu.make_async_remote_copy(
            src_ref=source,
            dst_ref=piece(k, way, part),
            send_sem=ring_send.at[way, k, part],
            recv_sem=ring_recv.at[way, k, part],
            device_id=towards[way],
            device_id_type=pl.DeviceIdType.MESH,
        )

    def to_sibling(source, target, send, recv):
        return pltpu.make_async_remote_copy(
            src_ref=source,
            dst_ref=target,
            send_sem=send,
            recv_sem=recv,
            device_id=sibling,
            device_id_type=pl.DeviceIdType.MESH,
        )

    small[0].wait()
    small[1].wait()
    x = patches[...].astype(F32)
    centre = x - jnp.mean(x, axis=-1, keepdims=True)
    variance = jnp.mean(centre * centre, axis=-1, keepdims=True)
    xg[0] = (centre * lax.rsqrt(variance + 1e-05) * ln_gain[...]).astype(BF16)

    pl.semaphore_wait(barrier, 3)
    share = to_sibling(xg.at[0], xs, sib_send, sib_recv)
    for h in range(2):
        for part in range(len(PARTS)):
            for way in range(2):
                hop(way, 1 + h, part, piece(0, h ^ way, part)).start()
        if h == 0:
            share.start()

    row_id = lax.broadcasted_iota(jnp.int32, (4 * HD, 4 * HD), 0) >> 6
    col_id = lax.broadcasted_iota(jnp.int32, (4 * HD, 4 * HD), 1) >> 6
    ones[...] = jnp.where(row_id == col_id, 1.0, 0.0).astype(BF16)
    m_ref[...] = jnp.full(m_ref.shape, -1e30, F32)
    l_ref[...] = jnp.zeros(l_ref.shape, F32)
    acc[...] = jnp.zeros(acc.shape, F32)
    qbd[...] = jnp.zeros(qbd.shape, BF16)

    def head_norm(columns, gain):
        parts = []
        for i in range(columns.shape[1] // (4 * HD)):
            block = columns[:, i * 4 * HD : (i + 1) * 4 * HD]
            total = dot((block * block).astype(BF16), ones[...])
            parts.append(block * lax.rsqrt(total * (1.0 / HD) + 1e-06))
        return jnp.concatenate(parts, axis=1) * gain

    small[2].wait()
    loads[0].wait()
    share.wait()
    for which, source in enumerate((xg.at[0], xs)):
        query = head_norm(dot(source[...], wq[...]), gains[0:1, :]) * (HD ** -0.5 * LOG2E)
        for j in range(pairs):
            block = query[:, j * 2 * HD : (j + 1) * 2 * HD].T.astype(BF16)
            for e in range(2):
                first = e * nq + which * rows
                qbd[j, e * HD : (e + 1) * HD, first : first + rows] = block[e * HD : (e + 1) * HD]
    loads[1].wait()
    loads[2].wait()

    def project(k):
        tokens = xg[k]
        values_t[...] = dot(tokens, wv[...]).astype(BF16).T
        keys[...] = head_norm(dot(tokens, wk[...]), gains[1:2, :]).astype(BF16)

    def attend(lo, hi, first, last, giving=False):
        spans = [slice(e * nq + first, e * nq + last) for e in range(2)]
        size = last - first

        def load(ref, j):
            return jnp.concatenate([ref[j, :, span] for span in spans], axis=1)

        shrinks = {}
        for j in range(lo, hi):
            scores = dot(keys[:, j * 2 * HD : (j + 1) * 2 * HD], load(qbd, j))
            old = load(m_ref, j)
            new = jnp.maximum(old, jnp.max(scores, axis=0, keepdims=True))
            shrinks[j] = jnp.exp2(old - new)
            exponent = jnp.exp2(scores - new)
            total = load(l_ref, j) * shrinks[j] + jnp.sum(exponent, axis=0, keepdims=True)
            for e, span in enumerate(spans):
                columns = slice(e * size, (e + 1) * size)
                if giving:
                    given_stats[j, 0, :, columns] = new[:, columns]
                    given_stats[j, 1, :, columns] = total[:, columns]
                else:
                    m_ref[j, :, span] = new[:, columns]
                    l_ref[j, :, span] = total[:, columns]
                weights[j, :, span] = exponent[:, columns].astype(BF16)
        for j in range(lo, hi):
            both = slice(2 * j * HD, 2 * (j + 1) * HD)
            joint = dot(values_t[both, :], load(weights, j)) if size <= 2 * HD else None
            for e, span in enumerate(spans):
                channels = slice((2 * j + e) * HD, (2 * j + e + 1) * HD)
                columns = slice(e * size, (e + 1) * size)
                if joint is None:
                    term = dot(values_t[channels, :], weights[j, :, span])
                else:
                    term = joint[e * HD : (e + 1) * HD, columns]
                value = acc[channels, first:last] * shrinks[j][:, columns] + term
                if giving:
                    given[j, e * HD : (e + 1) * HD, :] = value.astype(BF16)
                else:
                    acc[channels, first:last] = value

    def drain(k):
        for part in range(len(PARTS)):
            for way in range(2):
                hop(way, k, part, piece(k, way, part)).wait_send()

    def receive(k):
        for part in range(len(PARTS)):

            @pl.when((k < n - 1) | (part < len(PARTS) - 1))
            def _():
                for way in range(2):
                    hop(way, k, part, piece(k, way, part)).wait_recv()

                    @pl.when(k < n - 2)
                    def _():
                        hop(way, k + 2, part, piece(k, way, part)).start()

        @pl.when(k >= 2)
        def _():
            drain(k - 1)

    def step(k, carry):
        project(k)
        attend(0, pairs, 0, nq)
        receive(k + 1)
        return carry

    lax.fori_loop(0, n - 1, step, 0)

    def give(i, lo, hi):
        return (
            to_sibling(
                given_stats.at[lo:hi], came_stats.at[lo:hi], merge_send.at[0, i], merge_recv.at[0, i]
            ),
            to_sibling(given.at[lo:hi], came.at[lo:hi], merge_send.at[1, i], merge_recv.at[1, i]),
        )

    ends = [sum(GROUPS[:i]) * pairs // sum(GROUPS) for i in range(len(GROUPS) + 1)]
    groups = list(zip(ends, ends[1:]))
    early, late = slice(0, cuts[-2]), slice(cuts[-2], d)
    some_values[...] = dot(xg[n - 1, :, early], wv[early, :])
    some_keys[...] = dot(xg[n - 1, :, early], wk[early, :])
    for way in range(2):
        hop(way, n - 1, len(PARTS) - 1, piece(n - 1, way, len(PARTS) - 1)).wait_recv()
    tokens = xg[n - 1, :, late]
    keys[...] = head_norm(some_keys[...] + dot(tokens, wk[late, :]), gains[1:2, :]).astype(BF16)
    values_t[...] = (some_values[...] + dot(tokens, wv[late, :])).astype(BF16).T
    for i, (lo, hi) in enumerate(groups):
        attend(lo, hi, rows, nq, giving=True)
        for copy in reversed(give(i, lo, hi)):
            copy.start()

    attend(0, pairs, 0, rows)
    drain(n - 1)
    load_out.wait()
    total = None
    for i, (lo, hi) in enumerate(groups):
        for copy in give(i, lo, hi):
            copy.wait_recv()
        attended = []
        for j in range(lo, hi):
            heads = []
            for e in range(2):
                mine = slice(e * nq, e * nq + rows)
                here = slice(e * rows, (e + 1) * rows)
                m_own, m_came = m_ref[j, :, mine], came_stats[j, 0, :, here]
                m_all = jnp.maximum(m_own, m_came)
                own, other = jnp.exp2(m_own - m_all), jnp.exp2(m_came - m_all)
                inverse = 1.0 / (l_ref[j, :, mine] * own + came_stats[j, 1, :, here] * other)
                channels = slice((2 * j + e) * HD, (2 * j + e + 1) * HD)
                heads.append(
                    acc[channels, 0:rows] * (own * inverse)
                    + came[j, e * HD : (e + 1) * HD, :].astype(F32) * (other * inverse)
                )
            attended.append(jnp.concatenate(heads, axis=0).T.astype(BF16))
        part = dot(jnp.concatenate(attended, axis=1), wo[2 * lo * HD : 2 * hi * HD, :])
        total = part if total is None else total + part
    out[...] = total.astype(BF16)

    for i, (lo, hi) in enumerate(groups):
        for copy in give(i, lo, hi):
            copy.wait_send()


def per_device(patches, ln_gain, w_qkv, qk_gains, w_out):
    rows, d = patches.shape
    n = lax.axis_size("blk")
    nq = 2 * rows
    pairs = d // (2 * HD)
    hbm = pl.BlockSpec(memory_space=pltpu.HBM)
    operands = (patches, ln_gain.reshape(1, d), qk_gains, w_qkv, w_out)
    return pl.pallas_call(
        functools.partial(kernel, n, rows, d),
        out_shape=jax.ShapeDtypeStruct((rows, d), BF16),
        in_specs=[hbm] * len(operands),
        out_specs=pl.BlockSpec(memory_space=pltpu.VMEM),
        scratch_shapes=[
            pltpu.VMEM((rows, d), BF16),
            pltpu.VMEM((1, d), F32),
            pltpu.VMEM((2, d), F32),
            pltpu.VMEM((n, rows, d), BF16),
            pltpu.VMEM((rows, d), BF16),
            pltpu.VMEM((d, d), BF16),
            pltpu.VMEM((d, d), BF16),
            pltpu.VMEM((d, d), BF16),
            pltpu.VMEM((d, d), BF16),
            pltpu.VMEM((pairs, 2 * HD, 2 * nq), BF16),
            pltpu.VMEM((4 * HD, 4 * HD), BF16),
            pltpu.VMEM((rows, d), BF16),
            pltpu.VMEM((d, rows), BF16),
            pltpu.VMEM((pairs, rows, 2 * nq), BF16),
            pltpu.VMEM((pairs, 1, 2 * nq), F32),
            pltpu.VMEM((pairs, 1, 2 * nq), F32),
            pltpu.VMEM((d, nq), F32),
            pltpu.VMEM((rows, d), F32),
            pltpu.VMEM((rows, d), F32),
            pltpu.VMEM((pairs, 2 * HD, rows), BF16),
            pltpu.VMEM((pairs, 2 * HD, rows), BF16),
            pltpu.VMEM((pairs, 2, 1, nq), F32),
            pltpu.VMEM((pairs, 2, 1, nq), F32),
            pltpu.SemaphoreType.DMA((7,)),
            pltpu.SemaphoreType.DMA((2, n, len(PARTS))),
            pltpu.SemaphoreType.DMA((2, n, len(PARTS))),
            pltpu.SemaphoreType.DMA,
            pltpu.SemaphoreType.DMA,
            pltpu.SemaphoreType.DMA((2, len(GROUPS))),
            pltpu.SemaphoreType.DMA((2, len(GROUPS))),
        ],
        compiler_params=pltpu.CompilerParams(
            collective_id=0, has_side_effects=True, vmem_limit_bytes=48 << 20
        ),
    )(*(pltpu.with_memory_space_constraint(a, pltpu.HBM) for a in operands))


def solution(mesh):
    placed = (P(("group", "head", "blk"), None), P(), P(), P(), P())
    return jax.shard_map(
        per_device,
        mesh=mesh,
        in_specs=placed,
        out_specs=P(("group", "head", "blk"), None),
        check_vma=False,
    )
```
